32 devices in a mesh: ia: 4 (over z), ja: 4 (over y, x), ka: 2 (over core).
Axes of the slice: x: 2, y: 2, z: 4, core: 2. Of those that a mesh axis runs over, the one named last changes fastest.
Arguments:
- blocks: bfloat16 [4, 4, 4, 128, 128, 128], P('ia', 'ja', 'ka'), may hold values from -6 to 6
- coordinates: int32 [3, 4, 4, 4], P(None, 'ia', 'ja', 'ka'), may hold values from 0 to 3, as said below
- occupancy: int32 [4, 4, 4], P('ia', 'ja', 'ka'), may hold values from 0 to 1, as said below
- second_factor: bfloat16 [4, 512, 1024], P('ja', ('ia', 'ka')), may hold values from -12 to 12
- third_factor: bfloat16 [2, 512, 1024], P('ka', ('ia', 'ja')), may hold values from -0.0234375 to 0.0234375
- inverse_first: bfloat16 [1024, 1024], replicated
- inverse_second: bfloat16 [1024, 1024], replicated
Outputs:
- first_new: bfloat16 [4, 512, 1024], P('ia', ('ja', 'ka'))
- second_new: bfloat16 [4, 512, 1024], P('ja', ('ia', 'ka'))
The draws below stay inside these ranges and needn't reach their ends.
Inputs may be any that keep to these rules, and one draw needn't show every extreme that they name: `occupancy`: each device has two slots; its second slot is occupied only where its first is. A device with two blocks is followed along ka, cyclically, by a device with none. Some device holds two blocks. coordinates[0], [1], [2] of a slot are a block row among 4, a block row among 4 and a block layer among 4 of its device's ranges; the two slots of a device name different layers.
All inputs are finite; a program needn't handle non-finite values.
Results may differ from the reference program's by a relative error of at most 0.006.
Values may be sent and summed in bfloat16 or wider, within the bound.
A program may use at most 128 MiB of HBM per device.

```python
import jax
import jax.numpy as jnp
from jax import lax

R = 1024
BLK = 128
SLOTS = 2
IB = 4
JB = 4
KB = 4
N_IA = 4
N_JA = 4
N_KA = 2


def draw_occupancy(key, part):
    subkeys = jax.random.split(jax.random.fold_in(key, 31), 3)
    cycles = N_IA * N_JA
    draws_raw = jax.random.randint(subkeys[0], (cycles, N_KA), 0, 20)
    counts = jnp.where(draws_raw < 7, 0, jnp.where(draws_raw < 14, 1, 2))
    forced_cycle = jax.random.randint(subkeys[1], (), 0, cycles)
    forced_place = jax.random.randint(subkeys[2], (), 0, N_KA)
    cycle_ids = jnp.arange(cycles)[:, None]
    positions = jnp.arange(N_KA)[None, :]
    counts = jnp.where((cycle_ids == forced_cycle) & (positions == forced_place), 2, counts)
    counts = jnp.where((cycle_ids == forced_cycle) & (positions == (forced_place + N_KA - 1) % N_KA), 0, counts)
    previous = jnp.roll(counts, 1, axis=1)
    counts = jnp.where(previous == 2, 0, counts)
    occupied = jnp.stack([counts >= 1, counts >= 2], axis=-1).astype(jnp.int32)
    return occupied.reshape(N_IA, N_JA, N_KA * SLOTS)


def draw_coordinates(key, part):
    subkeys = jax.random.split(jax.random.fold_in(key, 41), 4)
    shape_dev = (N_IA, N_JA, N_KA, SLOTS)
    first_rows = jax.random.randint(subkeys[0], shape_dev, 0, IB)
    second_rows = jax.random.randint(subkeys[1], shape_dev, 0, JB)
    layer_first = jax.random.randint(subkeys[2], (N_IA, N_JA, N_KA), 0, KB)
    layer_step = jax.random.randint(subkeys[3], (N_IA, N_JA, N_KA), 1, KB)
    layers = jnp.stack([layer_first, (layer_first + layer_step) % KB], axis=-1)
    stacked = jnp.stack([first_rows, second_rows, layers], axis=0)
    return stacked.reshape(3, N_IA, N_JA, N_KA * SLOTS).astype(jnp.int32)


def gram_inverse(noise, diag_key):
    diagonal = jax.random.uniform(diag_key, (R,), jnp.float32, 0.4, 1.0)
    symmetric = (noise + noise.T) * (0.2 / (2.0 * R) ** 0.5)
    on_diagonal = jnp.arange(R)[:, None] == jnp.arange(R)[None, :]
    return symmetric + jnp.where(on_diagonal, diagonal[None, :], 0.0)


def draw_inverse_first(key, part):
    subkeys = jax.random.split(jax.random.fold_in(key, 11), 2)
    noise = jax.random.normal(subkeys[0], (R, R), jnp.float32)
    return gram_inverse(noise, subkeys[1]).astype(jnp.bfloat16)


def draw_inverse_second(key, part):
    subkeys = jax.random.split(jax.random.fold_in(key, 12), 2)
    noise = jax.random.normal(subkeys[0], (R, R), jnp.float32)
    return gram_inverse(noise, subkeys[1]).astype(jnp.bfloat16)


def shard_levels(key, extent, pieces, least, largest):
    gain, own = 1.0, jax.random.fold_in(key, 6)
    for dim, shards_of in pieces:
        draws = jnp.exp(jax.random.uniform(jax.random.fold_in(own, dim), (shards_of,), jnp.float32, least / len(pieces), largest / len(pieces)))
        gain = gain * jnp.repeat(draws, extent[dim] // shards_of).reshape([-1 if axis == dim else 1 for axis in range(len(extent))])
    return gain


def gaussian(rng, extent, width, most, cuts=(), kind=jnp.bfloat16):
    drawn = width * jax.random.normal(rng, extent, jnp.float32)
    if cuts:
        drawn = drawn * shard_levels(rng, extent, cuts, -0.22, 0.18)
    return jnp.clip(drawn, -most, most).astype(kind)


def setup_inputs(seed: int = 0) -> dict:
    keys = jax.random.split(jax.random.key(seed), 8)
    return {
        "blocks": gaussian(keys[0], (N_IA, N_JA, N_KA * SLOTS, BLK, BLK, BLK), 1.0, 6.0, ((0, 4), (1, 4), (2, 2))),
        "coordinates": draw_coordinates(jax.random.fold_in(keys[7], 71), 0),
        "occupancy": draw_occupancy(jax.random.fold_in(keys[7], 71), 0),
        "second_factor": gaussian(keys[3], (N_JA, JB * BLK, R), 2.0, 12.0, ((0, 4), (1, 8))),
        "third_factor": gaussian(keys[4], (N_KA, KB * BLK, R), 0.004, 0.0234375, ((0, 2), (1, 16))),
        "inverse_first": draw_inverse_first(jax.random.fold_in(keys[7], 71), 0),
        "inverse_second": draw_inverse_second(jax.random.fold_in(keys[7], 71), 0),
    }


def reference(blocks, coordinates, occupancy, second_factor, third_factor, inverse_first, inverse_second):
    total_slots = N_IA * N_JA * N_KA * SLOTS
    flat_blocks = blocks.reshape(total_slots, BLK, BLK, BLK)
    places = coordinates.reshape(3, total_slots)
    occupied = occupancy.reshape(total_slots)
    slot_ids = jnp.arange(total_slots, dtype=jnp.int32)
    first_plane = slot_ids // (N_JA * N_KA * SLOTS)
    second_plane = (slot_ids // (N_KA * SLOTS)) % N_JA
    third_plane = (slot_ids // SLOTS) % N_KA
    row_block = (first_plane * IB + places[0]).astype(jnp.int32)
    col_block = (second_plane * JB + places[1]).astype(jnp.int32)
    layer_block = (third_plane * KB + places[2]).astype(jnp.int32)
    second_table = second_factor.reshape(N_JA * JB * BLK, R)
    third_table = third_factor.reshape(N_KA * KB * BLK, R)

    def mode_sum(target_rows, own_block, left_block, left_table, swapped):
        def add_block(totals, slot_index):
            def include(carry):
                tensor_block = lax.dynamic_index_in_dim(flat_blocks, slot_index, 0, keepdims=False)
                if swapped:
                    tensor_block = jnp.transpose(tensor_block, (1, 0, 2))
                left_slab = lax.dynamic_slice_in_dim(left_table, left_block[slot_index] * BLK, BLK, 0)
                layer_slab = lax.dynamic_slice_in_dim(third_table, layer_block[slot_index] * BLK, BLK, 0)
                khatri = (left_slab[:, None, :].astype(jnp.float32) * layer_slab[None, :, :].astype(jnp.float32)).astype(jnp.bfloat16)
                product = jnp.dot(tensor_block.reshape(BLK, BLK * BLK), khatri.reshape(BLK * BLK, R), preferred_element_type=jnp.float32)
                row_start = own_block[slot_index] * BLK
                current = lax.dynamic_slice_in_dim(carry, row_start, BLK, 0)
                return lax.dynamic_update_slice_in_dim(carry, current + product, row_start, 0)
            return lax.cond(occupied[slot_index] > 0, include, lambda carry: carry, totals), None
        zeroed = jnp.zeros((target_rows, R), jnp.float32)
        result, unused = lax.scan(add_block, zeroed, slot_ids)
        return result

    first_sum = mode_sum(N_IA * IB * BLK, row_block, col_block, second_table, False)
    first_new = jnp.dot(first_sum.astype(jnp.bfloat16), inverse_first, preferred_element_type=jnp.float32).astype(jnp.bfloat16)
    second_sum = mode_sum(N_JA * JB * BLK, col_block, row_block, first_new, True)
    second_new = jnp.dot(second_sum.astype(jnp.bfloat16), inverse_second, preferred_element_type=jnp.float32).astype(jnp.bfloat16)
    return first_new.reshape(N_IA, IB * BLK, R), second_new.reshape(N_JA, JB * BLK, R)
```

```python
import functools

import jax
import jax.numpy as jnp
from jax import lax
from jax.experimental import pallas as pl
from jax.experimental.pallas import tpu as pltpu
from jax.sharding import PartitionSpec as P

IB = 4
JB = 4
TILES = 4
PARTS = 2
VMEM_LIMIT = 67043328
MESH = pl.DeviceIdType.MESH
AXES = ("ia", "ja", "ka")


def kernel(
    sizes,
    blocks,
    places_in,
    occupied_in,
    second_in,
    third_in,
    inverse_first,
    inverse_second,
    first_out,
    second_out,
    xbuf,
    inv1,
    inv2,
    meta_s,
    meta_r,
    cbuf,
    bbuf,
    slab_s,
    slab_r,
    cuse,
    buse,
    tbuf,
    oacc,
    d1s,
    d1r,
    keep1,
    p1s,
    p1r,
    own1,
    fr1,
    abuf,
    d2s,
    d2r,
    keep2,
    p2s,
    p2r,
    own2,
    fr2,
    places,
    occupied,
    local_sem,
    once_send,
    once_recv,
    z_send,
    z_recv,
    y_send,
    y_recv,
    k_send,
    k_recv,
):
    na, nb, nc = sizes
    tiles, edge, width = slab_s.shape
    rs, rt = bbuf.shape[3], cbuf.shape[3]
    sh1, sh2 = abuf.shape[3], own2.shape[1]
    a, b, c = (lax.axis_index(name) for name in AXES)
    sent = []

    def away(axis, d):
        n = sizes[AXES.index(axis)]
        me = (a, b, c)[AXES.index(axis)]
        return lax.rem(me + d, n)

    def send(src, dst, send_sem, recv_sem, axis, d):
        copy = pltpu.make_async_remote_copy(
            src_ref=src,
            dst_ref=dst,
            send_sem=send_sem,
            recv_sem=recv_sem,
            device_id={axis: away(axis, d)},
            device_id_type=MESH,
        )
        copy.start()
        sent.append(copy)
        return copy

    def cols(t):
        return pl.ds(t * width, width)

    local = []

    def local_copy(src, dst):
        copy = pltpu.make_async_copy(src, dst, local_sem.at[len(local)])
        copy.start()
        local.append(copy)
        return copy

    got_places = local_copy(places_in, places)
    got_occupied = local_copy(occupied_in, occupied)
    own_third = [
        local_copy(third_in.at[0, :, cols(t)], cbuf.at[t, a, b]) for t in range(tiles)
    ]
    own_second = [
        local_copy(second_in.at[0, :, cols(t)], bbuf.at[t, a, c]) for t in range(tiles)
    ]
    own_block = local_copy(blocks.at[0, 0, 0], xbuf.at[0])
    got_inv1 = local_copy(inverse_first, inv1)
    got_inv2 = local_copy(inverse_second, inv2)

    barrier = pltpu.get_barrier_semaphore()
    for axis, n in zip(AXES, sizes):
        for d in range(1, n):
            pl.semaphore_signal(
                barrier, inc=1, device_id={axis: away(axis, d)}, device_id_type=MESH
            )
    got_places.wait()
    got_occupied.wait()
    keep = occupied[0, 0, 0] > 0
    row0, col0, layer0 = (places[m, 0, 0, 0] for m in range(3))
    row1, col1, layer1 = (places[m, 0, 0, 1] for m in range(3))
    weight1 = jnp.where(occupied[0, 0, 1] > 0, 1.0, 0.0).astype(jnp.float32)
    for q in range(IB):
        value = jnp.where(row1 == q, weight1, 0.0)
        meta_s[pl.ds(q, 1), :] = jnp.full((1, width), value, jnp.float32)
    for q in range(JB):
        value = jnp.where(col1 == q, weight1, 0.0)
        meta_s[pl.ds(IB + q, 1), :] = jnp.full((1, width), value, jnp.float32)
    pl.semaphore_wait(barrier, (na - 1) + (nb - 1) + (nc - 1))

    def chosen(own_value, row):
        own = jnp.where(own_value, 1.0, 0.0).astype(jnp.float32)
        return jnp.where(keep, jnp.full((1, width), own, jnp.float32), meta_r[pl.ds(row, 1), :]) > 0.5

    def third_column(t):
        return [
            send(
                third_in.at[0, :, cols(t)],
                cbuf.at[t, a, b],
                z_send.at[0, t, d - 1],
                z_recv.at[0, t, d - 1],
                "ia",
                d,
            )
            for d in range(1, na)
        ]

    def second_column(t):
        return [
            send(
                second_in.at[0, :, cols(t)],
                bbuf.at[t, a, c],
                z_send.at[1, t, d - 1],
                z_recv.at[1, t, d - 1],
                "ia",
                d,
            )
            for d in range(1, na)
        ]

    third_z, second_z = {}, {}
    third_z[0] = third_column(0)
    block_copy = send(blocks.at[0, 0, 1], xbuf.at[1], once_send.at[0], once_recv.at[0], "ka", 1)
    meta_copy = send(meta_s, meta_r, once_send.at[1], once_recv.at[1], "ka", 1)
    for t in range(1, tiles):
        third_z[t] = third_column(t)
        second_z[t - 1] = second_column(t - 1)
    second_z[tiles - 1] = second_column(tiles - 1)

    third_y, second_k, slab_copy = {}, {}, {}

    def spread_third(t):
        own_third[t].wait()
        for copy in third_z[t]:
            copy.wait_recv()
        third_y[t] = [
            send(
                cbuf.at[t, :, b],
                cbuf.at[t, :, b],
                y_send.at[0, t, d - 1],
                y_recv.at[0, t, d - 1],
                "ja",
                d,
            )
            for d in range(1, nb)
        ]

    def spread_second(t):
        own_second[t].wait()
        for copy in second_z[t]:
            copy.wait_recv()
        second_k[t] = [
            send(
                bbuf.at[t, :, c],
                bbuf.at[t, :, c],
                k_send.at[0, t, d - 1],
                k_recv.at[0, t, d - 1],
                "ka",
                d,
            )
            for d in range(1, nc)
        ]

    def layer_piece(t, layer, piece):
        per = edge // rt
        total = na * nb * rt // edge
        value = None
        for q in range(total):
            s = q * per + piece
            rows = cbuf[t, s // nb, s % nb]
            value = rows if value is None else jnp.where(layer == q, rows, value)
        return value

    def pass_slab(t):
        for copy in third_y[t]:
            copy.wait_recv()
        for piece in range(edge // rt):
            slab_s[t, pl.ds(piece * rt, rt), :] = layer_piece(t, layer1, piece)
        slab_copy[t] = send(
            slab_s.at[t], slab_r.at[t], k_send.at[1, t, 0], k_recv.at[1, t, 0], "ka", 1
        )
        for piece in range(edge // rt):
            cuse[pl.ds(piece * rt, rt), :] = layer_piece(t, layer0, piece)

    def first_products(t):
        for copy in second_k[t]:
            copy.wait_recv()
        if t == 0:
            own_block.wait()
            block_copy.wait_recv()
            meta_copy.wait_recv()
        masks = [chosen(col0 == q, IB + q) for q in range(JB)]
        per = edge // rs
        for piece in range(per):
            value = jnp.zeros((rs, width), jnp.float32)
            for q in range(JB):
                s = q * per + piece
                rows = bbuf[t, s // nc, s % nc].astype(jnp.float32)
                value = jnp.where(masks[q], rows, value)
            buse[pl.ds(piece * rs, rs), :] = value
        slab_copy[t].wait_recv()
        cuse[...] = jnp.where(keep, cuse[...], slab_r[t])
        slot = jnp.where(keep, 0, 1)

        def eight(step, carry):
            base = pl.multiple_of(step * 8, 8)
            sums = []
            for u in range(8):
                product = jnp.dot(
                    xbuf[slot, base + u], cuse[...], preferred_element_type=jnp.float32
                )
                tbuf[t, base + u] = product.astype(jnp.bfloat16)
                sums.append(jnp.sum(product * buse[...], axis=0, keepdims=True))
            oacc[pl.ds(base, 8), :] = jnp.concatenate(sums, axis=0)
            return carry

        lax.fori_loop(0, edge // 8, eight, 0)

    def owned_piece(owner, rows, own_place, meta_row):
        start = owner * rows
        block = start // edge
        off = pl.multiple_of(start % edge, rows)
        mask = chosen(own_place == block, meta_row + block)
        return jnp.where(mask, oacc[pl.ds(off, rows), :], 0.0)

    def pair_sums(t, n, rows, own_place, meta_row, outgoing, arriving, kept, kind):
        copies = []
        for d in range(1, nc):
            for m in range(n):
                owner = m * nc + away("ka", d)
                outgoing[t, d - 1, m] = owned_piece(owner, rows, own_place, meta_row).astype(
                    jnp.bfloat16
                )
            copies.append(
                send(
                    outgoing.at[t, d - 1],
                    arriving.at[t, d - 1],
                    k_send.at[kind, t, d - 1],
                    k_recv.at[kind, t, d - 1],
                    "ka",
                    d,
                )
            )
        for m in range(n):
            kept[t, m] = owned_piece(m * nc + c, rows, own_place, meta_row)
        return copies

    def chip_sums(t, axis, n, copies, arriving, kept, outgoing, landing, own, sends, recvs, kind):
        for copy in copies:
            copy.wait_recv()
        started = []
        for d in range(n):
            m = away(axis, d)
            value = kept[t, m]
            for e in range(1, nc):
                value = value + arriving[t, e - 1, m].astype(jnp.float32)
            if d == 0:
                own[t] = value
            else:
                outgoing[t, d - 1] = value.astype(jnp.bfloat16)
                started.append(
                    send(
                        outgoing.at[t, d - 1],
                        landing.at[t, d - 1],
                        sends.at[kind, t, d - 1],
                        recvs.at[kind, t, d - 1],
                        axis,
                        d,
                    )
                )
        return started

    first_k, first_y = {}, {}

    def first_chip_sums(t):
        first_y[t] = chip_sums(
            t, "ja", nb, first_k[t], d1r, keep1, p1s, p1r, own1, y_send, y_recv, 1
        )

    spread_third(0)
    spread_second(0)
    for t in range(tiles):
        if t + 1 < tiles:
            spread_third(t + 1)
        pass_slab(t)
        if t:
            first_chip_sums(t - 1)
        first_products(t)
        first_k[t] = pair_sums(t, nb, sh1, row0, 0, d1s, d1r, keep1, 2)
        if t + 1 < tiles:
            spread_second(t + 1)
    first_chip_sums(tiles - 1)

    def gathered(t, copies, own, landing, n):
        for copy in copies:
            copy.wait_recv()
        value = own[t]
        for d in range(1, n):
            value = value + landing[t, d - 1].astype(jnp.float32)
        return value.astype(jnp.bfloat16)

    for t in range(tiles):
        fr1[:, cols(t)] = gathered(t, first_y[t], own1, p1r, nb)
    got_inv1.wait()
    new_y, new_k = {}, {}
    for t in range(tiles):
        value = jnp.dot(fr1[...], inv1[:, cols(t)], preferred_element_type=jnp.float32)
        value = value.astype(jnp.bfloat16)
        abuf[t, b, c] = value
        first_out[0, :, cols(t)] = value
        new_y[t] = [
            send(
                abuf.at[t, b, c],
                abuf.at[t, b, c],
                y_send.at[2, t, d - 1],
                y_recv.at[2, t, d - 1],
                "ja",
                d,
            )
            for d in range(1, nb)
        ]

    def spread_new(t):
        for copy in new_y[t]:
            copy.wait_recv()
        new_k[t] = [
            send(
                abuf.at[t, :, c],
                abuf.at[t, :, c],
                k_send.at[3, t, d - 1],
                k_recv.at[3, t, d - 1],
                "ka",
                d,
            )
            for d in range(1, nc)
        ]

    def second_products(t):
        for copy in new_k[t]:
            copy.wait_recv()
        masks = [chosen(row0 == q, q) for q in range(IB)]
        per = edge // sh1
        for piece in range(per):
            value = jnp.zeros((sh1, width), jnp.float32)
            for q in range(IB):
                s = q * per + piece
                rows = abuf[t, s // nc, s % nc].astype(jnp.float32)
                value = jnp.where(masks[q], rows, value)
            buse[pl.ds(piece * sh1, sh1), :] = value
        lanes = 128
        for lane in range(0, width, lanes):

            def eight(step, total):
                base = pl.multiple_of(step * 8, 8)
                rows = buse[pl.ds(base, 8), pl.ds(lane, lanes)]
                for u in range(8):
                    total = total + rows[u : u + 1] * tbuf[t, base + u, :, pl.ds(lane, lanes)].astype(
                        jnp.float32
                    )
                return total

            oacc[:, pl.ds(lane, lanes)] = lax.fori_loop(
                0, edge // 8, eight, jnp.zeros((edge, lanes), jnp.float32)
            )

    second_s, second_y = {}, {}

    def second_chip_sums(t):
        second_y[t] = chip_sums(
            t, "ia", na, second_s[t], d2r, keep2, p2s, p2r, own2, z_send, z_recv, 2
        )

    spread_new(0)
    for t in range(tiles):
        if t + 1 < tiles:
            spread_new(t + 1)
        second_products(t)
        second_s[t] = pair_sums(t, na, sh2, col0, IB, d2s, d2r, keep2, 4)
        if t:
            second_chip_sums(t - 1)
    second_chip_sums(tiles - 1)
    for t in range(tiles):
        fr2[:, cols(t)] = gathered(t, second_y[t], own2, p2r, na)
    got_inv2.wait()
    for t in range(tiles):
        value = jnp.dot(fr2[...], inv2[:, cols(t)], preferred_element_type=jnp.float32)
        second_out[0, :, cols(t)] = value.astype(jnp.bfloat16)
    for copy in sent:
        copy.wait_send()


def pair_kernel(
    sizes,
    blocks,
    places_in,
    occupied_in,
    second_in,
    third_in,
    inverse_first,
    inverse_second,
    first_out,
    second_out,
    xbuf,
    xturn,
    inv1,
    inv2,
    tz,
    ts,
    cg,
    bz,
    bs,
    br,
    pb,
    mine1,
    xs,
    xr,
    own1,
    fr1,
    sacc,
    srecv,
    own2,
    p2s,
    p2r,
    fr2,
    places,
    occupied,
    meta,
    local_sem,
    block_sem,
    meta_sems,
    tz_sems,
    far_sems,
    ts_sems,
    bz_sems,
    p1_sems,
    p2_sems,
    pair_sems,
):
    na, nb, nc = sizes
    tiles, rs, width = bs.shape
    parts, edge = tz_sems.shape[1], xbuf.shape[1]
    hr, wide = tz[0].shape[2:]
    half = edge // nc
    bf16, f32 = jnp.bfloat16, jnp.float32
    a, b, c = (lax.axis_index(name) for name in AXES)
    other = 1 - c
    sent, maybe_sent = [], []

    def send(src, dst, sems, place, **device_id):
        copy = pltpu.make_async_remote_copy(
            src_ref=src,
            dst_ref=dst,
            send_sem=sems.at[(0, *place)],
            recv_sem=sems.at[(1, *place)],
            device_id=device_id,
            device_id_type=MESH,
        )
        copy.start()
        sent.append(copy)
        return copy

    def arrival(dst, sem):
        return pltpu.make_async_remote_copy(
            src_ref=dst, dst_ref=dst, send_sem=sem, recv_sem=sem, device_id={"ka": other}, device_id_type=MESH
        )

    first, last = a == 0, a == na - 1
    inner = jnp.logical_and(a > 0, a < na - 1)
    far_piece = jnp.where(a == 1, na - 1, 0)
    far_dest = jnp.where(a == 1, 0, na - 1)

    def reaches(d):
        return jnp.logical_not(last if d == 1 else first) if d in (1, na - 1) else None

    def hears(d):
        return jnp.logical_not(first if d == 1 else last) if d in (1, na - 1) else None

    def under(condition, function):
        if condition is None:
            function()
        else:
            pl.when(condition)(function)

    def send_if(condition, src, dst, sems, place, **device_id):
        copy = pltpu.make_async_remote_copy(
            src_ref=src,
            dst_ref=dst,
            send_sem=sems.at[(0, *place)],
            recv_sem=sems.at[(1, *place)],
            device_id=device_id,
            device_id_type=MESH,
        )
        under(condition, copy.start)
        maybe_sent.append((condition, copy))

    def cols(t):
        return pl.ds(t * width, width)

    def wides(t):
        return pl.ds(t * wide, wide)

    def turn(me, d, n):
        return lax.rem(me + d, n)

    local = []

    def local_copy(src, dst):
        copy = pltpu.make_async_copy(src, dst, local_sem.at[len(local)])
        copy.start()
        local.append(copy)
        return copy

    def third_half(p, t):
        return third_in.at[0, pl.ds(pl.multiple_of(p * hr, hr), hr), wides(t)]

    barrier = pltpu.get_barrier_semaphore()
    peers = [{"ia": turn(a, d, na), "ka": turn(c, e, nc)} for d in range(na) for e in range(nc) if d or e]
    peers += [{"ja": turn(b, d, nb), "ka": turn(c, e, nc)} for d in range(1, nb) for e in range(nc)]
    for peer in peers:
        pl.semaphore_signal(barrier, inc=1, device_id=peer, device_id_type=MESH)

    got_places = local_copy(places_in, places)
    got_occupied = local_copy(occupied_in, occupied)
    own_third = [local_copy(third_half(c, t), tz[t].at[a, c]) for t in range(parts)]
    own_second = [local_copy(second_in.at[0, :, cols(t)], bz[t].at[a]) for t in range(tiles)]
    own_block = local_copy(blocks.at[0, 0, 0], xbuf.at[0])
    got_inv1 = local_copy(inverse_first, inv1)
    got_inv2 = local_copy(inverse_second, inv2)
    got_places.wait()
    got_occupied.wait()
    for slot in range(2):
        for m in range(3):
            meta[b, c, 4 * slot + m] = places[0, 0, slot, m]
        meta[b, c, 4 * slot + 3] = occupied[0, 0, slot]
    pl.semaphore_wait(barrier, len(peers))

    def third_column(t):
        for d in [*range(1, na), 0]:
            for e in range(nc):
                if d or e:
                    send_if(
                        reaches(d),
                        third_half(turn(c, e, nc), t),
                        tz[t].at[a, c],
                        tz_sems,
                        (t, d, e),
                        ia=turn(a, d, na),
                        ka=turn(c, e, nc),
                    )

    def third_near(t):
        own_third[t].wait()
        for d in [*range(1, na), 0]:
            for e in range(nc):
                if d or e:
                    under(hears(d), arrival(tz[t].at[a, c], tz_sems.at[1, t, d, e]).wait_recv)
        send_if(inner, tz[t].at[far_piece], tz[t].at[far_piece], far_sems, (0, t), ia=far_dest)

    def third_far(t):
        far = arrival(tz[t].at[na - 1], far_sems.at[1, 0, t])
        under(jnp.logical_not(inner), far.wait_recv)

    def second_column(t):
        for d in range(1, na):
            send_if(
                reaches(d),
                second_in.at[0, :, cols(t)],
                bz[t].at[a],
                bz_sems,
                (t, d - 1),
                ia=turn(a, d, na),
            )

    def second_near(t):
        own_second[t].wait()
        for d in range(1, na):
            under(hears(d), arrival(bz[t].at[a], bz_sems.at[1, t, d - 1]).wait_recv)
        send_if(inner, bz[t].at[far_piece], bz[t].at[far_piece], far_sems, (1, t), ia=far_dest)

    def second_far(t):
        far = arrival(bz[t].at[na - 1], far_sems.at[1, 1, t])
        under(jnp.logical_not(inner), far.wait_recv)

    meta_copies = [
        send(
            meta.at[b, c],
            meta.at[b, c],
            meta_sems,
            (d, e),
            ja=turn(b, d, nb),
            ka=turn(c, e, nc),
        )
        for d in range(nb)
        for e in range(nc)
        if d or e
    ]
    for t in range(parts):
        third_column(t)
    block_copy = send(blocks.at[0, 0, 1], xbuf.at[1], block_sem, (), ka=other)
    second_column(0)

    for copy in meta_copies:
        copy.wait_recv()

    def work(bb, cc):
        keep = meta[bb, cc, 3] > 0
        row, col, layer = (jnp.where(keep, meta[bb, cc, m], meta[bb, 1 - cc, 4 + m]) for m in range(3))
        return row, col, layer, jnp.where(keep, cc, 1 - cc), jnp.where(keep, 1, meta[bb, 1 - cc, 7])

    row_own, col_own, _, kept, valid_own = work(b, c)
    row_oth, col_oth, _, _, valid_oth = work(b, other)
    slot = jnp.where(kept == c, 0, 1)

    third_y = {}

    def pass_third(t):
        third_far(t)
        copies = []
        for d in range(nb):
            for e in range(nc):
                bb, cc = turn(b, d, nb), turn(c, e, nc)
                _, _, layer, span, _ = work(bb, cc)
                rows = tz[t][layer, span]
                if d or e:
                    ts[d, e, :, wides(t)] = rows
                    copies.append(
                        send(
                            ts.at[d, e, :, wides(t)],
                            cg.at[b, c, :, wides(t)],
                            ts_sems,
                            (t, d, e),
                            ja=bb,
                            ka=cc,
                        )
                    )
                else:
                    cg[b, c, :, wides(t)] = rows
        third_y[t] = copies

    ahead = [*range(1, tiles)]

    def more():
        if ahead:
            second_column(ahead.pop(0))

    for t in range(parts):
        third_near(t)
        if t == 0:
            more()
        pass_third(t)
    second_near(0)
    more()

    own_block.wait()
    block_copy.wait_recv()

    sub = 16

    def swap(step, carry):
        i0 = pl.multiple_of(step // (edge // sub) * sub, sub)
        j0 = pl.multiple_of(step % (edge // sub) * sub, sub)
        piece = xbuf[slot, pl.ds(i0, sub), pl.ds(j0, sub), :]
        xturn[pl.ds(j0, sub), pl.ds(i0, sub), :] = jnp.swapaxes(piece, 0, 1)
        return carry

    lax.fori_loop(0, (edge // sub) ** 2, swap, 0)

    def layers(t):
        return cg[:, :, :, cols(t)].reshape(edge, width)

    def halves(own, received):
        low = jnp.where(c == 0, own, received)
        high = jnp.where(c == 0, received, own)
        return jnp.concatenate([low, high], axis=0)

    def product(rows, layer_rows, pages):
        left = jnp.concatenate(pages, axis=1)
        right = jnp.concatenate([rows[u : u + 1] * layer_rows for u in range(edge)], axis=0)
        return jnp.dot(left, right, preferred_element_type=f32)

    own_rows = pl.ds(pl.multiple_of(c * half, half), half)
    other_rows = pl.ds(pl.multiple_of(other * half, half), half)

    def swap_half(t, acc, received, kind):
        return send(acc.at[t, other_rows], received.at[t], pair_sems, (kind, t), ka=other)

    def buckets(t, copy, acc, received, place_own, place_oth, me, axis, n, own, outgoing, landing, sems):
        copy.wait_recv()
        mine, theirs = acc[t, own_rows], received[t]
        copies = []
        for d in [*range(1, n), 0]:
            q = turn(me, d, n)
            value = jnp.where((place_own == q) & (valid_own > 0), mine, 0.0) + jnp.where(
                (place_oth == q) & (valid_oth > 0), theirs, 0.0
            )
            if d:
                outgoing[t, d - 1] = value.astype(bf16)
                copies.append(
                    send(outgoing.at[t, d - 1], landing.at[t, d - 1], sems, (t, d - 1), **{axis: q})
                )
            else:
                own[t] = value
        return copies

    def gathered(t, copies, own, landing, n):
        for copy in copies:
            copy.wait_recv()
        value = own[t]
        for d in range(1, n):
            value = value + landing[t, d - 1].astype(f32)
        return value.astype(bf16)

    second_k, first_y, first_k, second_s, second_y = {}, {}, {}, {}, {}
    in_plane = [work(bb, c) for bb in range(nb)]

    def pass_second(t):
        second_far(t)
        bs[t] = bz[t][col_oth]
        second_k[t] = send(bs.at[t], br.at[t], pair_sems, (0, t), ka=other)

    def first_products(t):
        second_k[t].wait_recv()
        sums = product(halves(bz[t][col_own], br[t]), layers(t), [xturn[j] for j in range(edge)])
        pb[t][b] = sums.astype(bf16)
        first_y[t] = [
            send(pb[t].at[b], pb[t].at[b], p1_sems, (t, d - 1), ja=turn(b, d, nb))
            for d in range(1, nb)
        ]

    def first_sums(t):
        for copy in first_y[t]:
            copy.wait_recv()

        def rows_of(place, rows):
            total = None
            for bb in range(nb):
                row, _, _, _, valid = in_plane[bb]
                chosen = jnp.logical_and(row == place, valid > 0)
                value = jnp.where(chosen, pb[t][bb, rows].astype(f32), 0.0)
                total = value if total is None else total + value
            return total

        xs[t, pl.ds(0, edge)] = rows_of(row_oth, pl.ds(0, edge))
        xs[t, pl.ds(edge, half)] = rows_of(b, other_rows)
        first_k[t] = send(xs.at[t], xr.at[t], pair_sems, (1, t), ka=other)
        mine1[t] = rows_of(row_own, pl.ds(0, edge))
        own1[t] = rows_of(b, own_rows)

    def first_rows(t):
        first_k[t].wait_recv()
        fr1[pl.ds(0, edge), cols(t)] = (mine1[t] + xr[t, pl.ds(0, edge)]).astype(bf16)
        fr1[pl.ds(edge, half), cols(t)] = (own1[t] + xr[t, pl.ds(edge, half)]).astype(bf16)

    pass_second(0)
    for part in range(parts):
        for copy in third_y[part]:
            copy.wait_recv()
    for t in range(tiles):
        if t + 1 < tiles:
            second_near(t + 1)
            more()
        first_products(t)
        if t + 1 < tiles:
            pass_second(t + 1)
        if t:
            first_sums(t - 1)
        if t > 1:
            first_rows(t - 2)
    first_sums(tiles - 1)
    for t in range(max(tiles - 2, 0), tiles):
        first_rows(t)
    got_inv1.wait()

    def second_buckets(t):
        second_y[t] = buckets(
            t, second_s[t], sacc, srecv, col_own, col_oth, a, "ia", na, own2, p2s, p2r, p2_sems
        )

    for t in range(tiles):
        value = jnp.dot(fr1[...], inv1[:, cols(t)], preferred_element_type=f32).astype(bf16)
        first_out[0, :, cols(t)] = value[edge:]
        sacc[t] = product(value[:edge], layers(t), [xbuf[slot, i] for i in range(edge)])
        second_s[t] = swap_half(t, sacc, srecv, 2)
        if t:
            second_buckets(t - 1)
    second_buckets(tiles - 1)
    for t in range(tiles):
        fr2[:, cols(t)] = gathered(t, second_y[t], own2, p2r, na)
    got_inv2.wait()
    for t in range(tiles):
        value = jnp.dot(fr2[...], inv2[:, cols(t)], preferred_element_type=f32)
        second_out[0, :, cols(t)] = value.astype(bf16)
    for copy in sent:
        copy.wait_send()
    for condition, copy in maybe_sent:
        under(condition, copy.wait_send)


def pair_call(sizes, blocks, coordinates, occupancy, second_factor, third_factor, inverse_first, inverse_second):
    na, nb, nc = sizes
    edge, rank = blocks.shape[-1], inverse_first.shape[0]
    tiles, parts = TILES, PARTS
    width = rank // tiles
    rs, hr = second_factor.shape[1], third_factor.shape[1] // nc
    half = edge // nc
    bf16, f32 = jnp.bfloat16, jnp.float32
    dma = pltpu.SemaphoreType.DMA
    vmem = pl.BlockSpec(memory_space=pltpu.VMEM)
    anywhere = pl.BlockSpec(memory_space=pl.ANY)
    places = jnp.transpose(coordinates, (1, 2, 3, 0))

    def sums(n):
        return [
            pltpu.VMEM((tiles, half, width), f32),
            pltpu.VMEM((tiles, n - 1, half, width), bf16),
            pltpu.VMEM((tiles, n - 1, half, width), bf16),
            pltpu.VMEM((half, rank), bf16),
        ]

    def swapped():
        return [pltpu.VMEM((tiles, edge, width), f32), pltpu.VMEM((tiles, half, width), f32)]

    def one_half():
        return [pltpu.VMEM((tiles, half, width), bf16)] * 2

    scratch = [
        pltpu.VMEM((2, edge, edge, edge), bf16),
        pltpu.VMEM((edge, edge, edge), bf16),
        pltpu.VMEM((rank, rank), bf16),
        pltpu.VMEM((rank, rank), bf16),
        (pltpu.VMEM((na, nc, hr, rank // parts), bf16),) * parts,
        pltpu.VMEM((nb, nc, hr, rank), bf16),
        pltpu.VMEM((nb, nc, hr, rank), bf16),
        (pltpu.VMEM((na, rs, width), bf16),) * tiles,
        *one_half(),
        (pltpu.VMEM((nb, edge, width), bf16),) * tiles,
        pltpu.VMEM((tiles, edge, width), f32),
        pltpu.VMEM((tiles, edge + half, width), f32),
        pltpu.VMEM((tiles, edge + half, width), f32),
        pltpu.VMEM((tiles, half, width), f32),
        pltpu.VMEM((edge + half, rank), bf16),
        *swapped(),
        *sums(na),
        pltpu.SMEM(places.shape, jnp.int32),
        pltpu.SMEM(occupancy.shape, jnp.int32),
        pltpu.SMEM((nb, nc, 8), jnp.int32),
        dma((parts + tiles + 5,)),
        dma((2,)),
        dma((2, nb, nc)),
        dma((2, parts, na, nc)),
        dma((2, 2, max(parts, tiles))),
        dma((2, parts, nb, nc)),
        dma((2, tiles, na - 1)),
        dma((2, tiles, nb - 1)),
        dma((2, tiles, na - 1)),
        dma((2, 3, tiles)),
    ]
    return pl.pallas_call(
        functools.partial(pair_kernel, sizes),
        name="als_pair",
        out_shape=(
            jax.ShapeDtypeStruct((1, half, rank), bf16),
            jax.ShapeDtypeStruct((1, half, rank), bf16),
        ),
        in_specs=[anywhere, anywhere, anywhere, vmem, vmem, anywhere, anywhere],
        out_specs=(vmem, vmem),
        scratch_shapes=scratch,
        compiler_params=pltpu.CompilerParams(
            collective_id=0, has_side_effects=True, vmem_limit_bytes=VMEM_LIMIT
        ),
    )(blocks, places, occupancy, second_factor, third_factor, inverse_first, inverse_second)


def pairs_fit(sizes, blocks, second_factor, third_factor):
    na, nb, nc = sizes
    edge = blocks.shape[-1]
    third_rows = third_factor.shape[1]
    return (
        nc == 2
        and na == JB
        and nb == IB
        and second_factor.shape[1] * nc == edge
        and third_rows * nb == edge
        and third_rows % (16 * nc) == 0
    )


def general_call(
    sizes,
    blocks,
    coordinates,
    occupancy,
    second_factor,
    third_factor,
    inverse_first,
    inverse_second,
):
    na, nb, nc = sizes
    edge, rank = blocks.shape[-1], inverse_first.shape[0]
    tiles = TILES
    width = rank // tiles
    rs, rt = second_factor.shape[1], third_factor.shape[1]
    sh1, sh2 = IB * edge // (nb * nc), JB * edge // (na * nc)
    bf16, f32 = jnp.bfloat16, jnp.float32
    dma = pltpu.SemaphoreType.DMA
    widest_k = max(nc - 1, 1)
    vmem = pl.BlockSpec(memory_space=pltpu.VMEM)
    anywhere = pl.BlockSpec(memory_space=pl.ANY)
    scratch = [
        pltpu.VMEM((2, edge, edge, edge), bf16),
        pltpu.VMEM((rank, rank), bf16),
        pltpu.VMEM((rank, rank), bf16),
        pltpu.VMEM((IB + JB, width), f32),
        pltpu.VMEM((IB + JB, width), f32),
        pltpu.VMEM((tiles, na, nb, rt, width), bf16),
        pltpu.VMEM((tiles, na, nc, rs, width), bf16),
        pltpu.VMEM((tiles, edge, width), bf16),
        pltpu.VMEM((tiles, edge, width), bf16),
        pltpu.VMEM((edge, width), bf16),
        pltpu.VMEM((edge, width), f32),
        pltpu.VMEM((tiles, edge, edge, width), bf16),
        pltpu.VMEM((edge, width), f32),
        pltpu.VMEM((tiles, nc - 1, nb, sh1, width), bf16),
        pltpu.VMEM((tiles, nc - 1, nb, sh1, width), bf16),
        pltpu.VMEM((tiles, nb, sh1, width), f32),
        pltpu.VMEM((tiles, nb - 1, sh1, width), bf16),
        pltpu.VMEM((tiles, nb - 1, sh1, width), bf16),
        pltpu.VMEM((tiles, sh1, width), f32),
        pltpu.VMEM((sh1, rank), bf16),
        pltpu.VMEM((tiles, nb, nc, sh1, width), bf16),
        pltpu.VMEM((tiles, nc - 1, na, sh2, width), bf16),
        pltpu.VMEM((tiles, nc - 1, na, sh2, width), bf16),
        pltpu.VMEM((tiles, na, sh2, width), f32),
        pltpu.VMEM((tiles, na - 1, sh2, width), bf16),
        pltpu.VMEM((tiles, na - 1, sh2, width), bf16),
        pltpu.VMEM((tiles, sh2, width), f32),
        pltpu.VMEM((sh2, rank), bf16),
        pltpu.SMEM(coordinates.shape, jnp.int32),
        pltpu.SMEM(occupancy.shape, jnp.int32),
        dma((2 * tiles + 5,)),
        dma((2,)),
        dma((2,)),
        dma((3, tiles, na - 1)),
        dma((3, tiles, na - 1)),
        dma((3, tiles, nb - 1)),
        dma((3, tiles, nb - 1)),
        dma((5, tiles, widest_k)),
        dma((5, tiles, widest_k)),
    ]
    return pl.pallas_call(
        functools.partial(kernel, sizes),
        name="als",
        out_shape=(
            jax.ShapeDtypeStruct((1, sh1, rank), bf16),
            jax.ShapeDtypeStruct((1, sh2, rank), bf16),
        ),
        in_specs=[anywhere, anywhere, anywhere, vmem, vmem, anywhere, anywhere],
        out_specs=(vmem, vmem),
        scratch_shapes=scratch,
        compiler_params=pltpu.CompilerParams(
            collective_id=0, has_side_effects=True, vmem_limit_bytes=67043328
        ),
    )(blocks, coordinates, occupancy, second_factor, third_factor, inverse_first, inverse_second)


def body(sizes, *args):
    blocks, second_factor, third_factor = args[0], args[3], args[4]
    vmem = pl.BlockSpec(memory_space=pltpu.VMEM)
    call = pair_call if pairs_fit(sizes, blocks, second_factor, third_factor) else general_call
    results = call(sizes, *args)
    return pl.pallas_call(
        hand_over,
        name="hand_over",
        out_shape=tuple(jax.ShapeDtypeStruct(x.shape, x.dtype) for x in results),
        in_specs=[vmem, vmem],
        out_specs=(vmem, vmem),
    )(*results)


def hand_over(first_in, second_in, first_out, second_out):
    first_out[...] = first_in[...]
    second_out[...] = second_in[...]


def solution(mesh):
    sizes = tuple(mesh.shape[name] for name in AXES)
    in_specs = (
        P("ia", "ja", "ka", None, None, None),
        P(None, "ia", "ja", "ka"),
        P("ia", "ja", "ka"),
        P("ja", ("ia", "ka"), None),
        P("ka", ("ia", "ja"), None),
        P(),
        P(),
    )
    out_specs = (P("ia", ("ja", "ka"), None), P("ja", ("ia", "ka"), None))
    return jax.shard_map(
        functools.partial(body, sizes),
        mesh=mesh,
        in_specs=in_specs,
        out_specs=out_specs,
        check_vma=False,
    )
```

```python
import functools

import jax
import jax.numpy as jnp
from jax import lax
from jax.experimental import pallas as pl
from jax.experimental.pallas import tpu as pltpu
from jax.sharding import PartitionSpec as P

IB = 4
JB = 4
TILES = 4
PAIR_TILES = 2
PARTS = 1
VMEM_LIMIT = 67043328
MESH = pl.DeviceIdType.MESH
AXES = ("ia", "ja", "ka")


def kernel(
    sizes,
    blocks,
    places_in,
    occupied_in,
    second_in,
    third_in,
    inverse_first,
    inverse_second,
    first_out,
    second_out,
    xbuf,
    inv1,
    inv2,
    meta_s,
    meta_r,
    cbuf,
    bbuf,
    slab_s,
    slab_r,
    cuse,
    buse,
    tbuf,
    oacc,
    d1s,
    d1r,
    keep1,
    p1s,
    p1r,
    own1,
    fr1,
    abuf,
    d2s,
    d2r,
    keep2,
    p2s,
    p2r,
    own2,
    fr2,
    places,
    occupied,
    local_sem,
    once_send,
    once_recv,
    z_send,
    z_recv,
    y_send,
    y_recv,
    k_send,
    k_recv,
):
    na, nb, nc = sizes
    tiles, edge, width = slab_s.shape
    rs, rt = bbuf.shape[3], cbuf.shape[3]
    sh1, sh2 = abuf.shape[3], own2.shape[1]
    a, b, c = (lax.axis_index(name) for name in AXES)
    sent = []

    def away(axis, d):
        n = sizes[AXES.index(axis)]
        me = (a, b, c)[AXES.index(axis)]
        return lax.rem(me + d, n)

    def send(src, dst, send_sem, recv_sem, axis, d):
        copy = pltpu.make_async_remote_copy(
            src_ref=src,
            dst_ref=dst,
            send_sem=send_sem,
            recv_sem=recv_sem,
            device_id={axis: away(axis, d)},
            device_id_type=MESH,
        )
        copy.start()
        sent.append(copy)
        return copy

    def cols(t):
        return pl.ds(t * width, width)

    local = []

    def local_copy(src, dst):
        copy = pltpu.make_async_copy(src, dst, local_sem.at[len(local)])
        copy.start()
        local.append(copy)
        return copy

    got_places = local_copy(places_in, places)
    got_occupied = local_copy(occupied_in, occupied)
    own_third = [
        local_copy(third_in.at[0, :, cols(t)], cbuf.at[t, a, b]) for t in range(tiles)
    ]
    own_second = [
        local_copy(second_in.at[0, :, cols(t)], bbuf.at[t, a, c]) for t in range(tiles)
    ]
    own_block = local_copy(blocks.at[0, 0, 0], xbuf.at[0])
    got_inv1 = local_copy(inverse_first, inv1)
    got_inv2 = local_copy(inverse_second, inv2)

    barrier = pltpu.get_barrier_semaphore()
    for axis, n in zip(AXES, sizes):
        for d in range(1, n):
            pl.semaphore_signal(
                barrier, inc=1, device_id={axis: away(axis, d)}, device_id_type=MESH
            )
    got_places.wait()
    got_occupied.wait()
    keep = occupied[0, 0, 0] > 0
    row0, col0, layer0 = (places[m, 0, 0, 0] for m in range(3))
    row1, col1, layer1 = (places[m, 0, 0, 1] for m in range(3))
    weight1 = jnp.where(occupied[0, 0, 1] > 0, 1.0, 0.0).astype(jnp.float32)
    for q in range(IB):
        value = jnp.where(row1 == q, weight1, 0.0)
        meta_s[pl.ds(q, 1), :] = jnp.full((1, width), value, jnp.float32)
    for q in range(JB):
        value = jnp.where(col1 == q, weight1, 0.0)
        meta_s[pl.ds(IB + q, 1), :] = jnp.full((1, width), value, jnp.float32)
    pl.semaphore_wait(barrier, (na - 1) + (nb - 1) + (nc - 1))

    def chosen(own_value, row):
        own = jnp.where(own_value, 1.0, 0.0).astype(jnp.float32)
        return jnp.where(keep, jnp.full((1, width), own, jnp.float32), meta_r[pl.ds(row, 1), :]) > 0.5

    def third_column(t):
        return [
            send(
                third_in.at[0, :, cols(t)],
                cbuf.at[t, a, b],
                z_send.at[0, t, d - 1],
                z_recv.at[0, t, d - 1],
                "ia",
                d,
            )
            for d in range(1, na)
        ]

    def second_column(t):
        return [
            send(
                second_in.at[0, :, cols(t)],
                bbuf.at[t, a, c],
                z_send.at[1, t, d - 1],
                z_recv.at[1, t, d - 1],
                "ia",
                d,
            )
            for d in range(1, na)
        ]

    third_z, second_z = {}, {}
    third_z[0] = third_column(0)
    block_copy = send(blocks.at[0, 0, 1], xbuf.at[1], once_send.at[0], once_recv.at[0], "ka", 1)
    meta_copy = send(meta_s, meta_r, once_send.at[1], once_recv.at[1], "ka", 1)
    for t in range(1, tiles):
        third_z[t] = third_column(t)
        second_z[t - 1] = second_column(t - 1)
    second_z[tiles - 1] = second_column(tiles - 1)

    third_y, second_k, slab_copy = {}, {}, {}

    def spread_third(t):
        own_third[t].wait()
        for copy in third_z[t]:
            copy.wait_recv()
        third_y[t] = [
            send(
                cbuf.at[t, :, b],
                cbuf.at[t, :, b],
                y_send.at[0, t, d - 1],
                y_recv.at[0, t, d - 1],
                "ja",
                d,
            )
            for d in range(1, nb)
        ]

    def spread_second(t):
        own_second[t].wait()
        for copy in second_z[t]:
            copy.wait_recv()
        second_k[t] = [
            send(
                bbuf.at[t, :, c],
                bbuf.at[t, :, c],
                k_send.at[0, t, d - 1],
                k_recv.at[0, t, d - 1],
                "ka",
                d,
            )
            for d in range(1, nc)
        ]

    def layer_piece(t, layer, piece):
        per = edge // rt
        total = na * nb * rt // edge
        value = None
        for q in range(total):
            s = q * per + piece
            rows = cbuf[t, s // nb, s % nb]
            value = rows if value is None else jnp.where(layer == q, rows, value)
        return value

    def pass_slab(t):
        for copy in third_y[t]:
            copy.wait_recv()
        for piece in range(edge // rt):
            slab_s[t, pl.ds(piece * rt, rt), :] = layer_piece(t, layer1, piece)
        slab_copy[t] = send(
            slab_s.at[t], slab_r.at[t], k_send.at[1, t, 0], k_recv.at[1, t, 0], "ka", 1
        )
        for piece in range(edge // rt):
            cuse[pl.ds(piece * rt, rt), :] = layer_piece(t, layer0, piece)

    def first_products(t):
        for copy in second_k[t]:
            copy.wait_recv()
        if t == 0:
            own_block.wait()
            block_copy.wait_recv()
            meta_copy.wait_recv()
        masks = [chosen(col0 == q, IB + q) for q in range(JB)]
        per = edge // rs
        for piece in range(per):
            value = jnp.zeros((rs, width), jnp.float32)
            for q in range(JB):
                s = q * per + piece
                rows = bbuf[t, s // nc, s % nc].astype(jnp.float32)
                value = jnp.where(masks[q], rows, value)
            buse[pl.ds(piece * rs, rs), :] = value
        slab_copy[t].wait_recv()
        cuse[...] = jnp.where(keep, cuse[...], slab_r[t])
        slot = jnp.where(keep, 0, 1)

        def eight(step, carry):
            base = pl.multiple_of(step * 8, 8)
            sums = []
            for u in range(8):
                product = jnp.dot(
                    xbuf[slot, base + u], cuse[...], preferred_element_type=jnp.float32
                )
                tbuf[t, base + u] = product.astype(jnp.bfloat16)
                sums.append(jnp.sum(product * buse[...], axis=0, keepdims=True))
            oacc[pl.ds(base, 8), :] = jnp.concatenate(sums, axis=0)
            return carry

        lax.fori_loop(0, edge // 8, eight, 0)

    def owned_piece(owner, rows, own_place, meta_row):
        start = owner * rows
        block = start // edge
        off = pl.multiple_of(start % edge, rows)
        mask = chosen(own_place == block, meta_row + block)
        return jnp.where(mask, oacc[pl.ds(off, rows), :], 0.0)

    def pair_sums(t, n, rows, own_place, meta_row, outgoing, arriving, kept, kind):
        copies = []
        for d in range(1, nc):
            for m in range(n):
                owner = m * nc + away("ka", d)
                outgoing[t, d - 1, m] = owned_piece(owner, rows, own_place, meta_row).astype(
                    jnp.bfloat16
                )
            copies.append(
                send(
                    outgoing.at[t, d - 1],
                    arriving.at[t, d - 1],
                    k_send.at[kind, t, d - 1],
                    k_recv.at[kind, t, d - 1],
                    "ka",
                    d,
                )
            )
        for m in range(n):
            kept[t, m] = owned_piece(m * nc + c, rows, own_place, meta_row)
        return copies

    def chip_sums(t, axis, n, copies, arriving, kept, outgoing, landing, own, sends, recvs, kind):
        for copy in copies:
            copy.wait_recv()
        started = []
        for d in range(n):
            m = away(axis, d)
            value = kept[t, m]
            for e in range(1, nc):
                value = value + arriving[t, e - 1, m].astype(jnp.float32)
            if d == 0:
                own[t] = value
            else:
                outgoing[t, d - 1] = value.astype(jnp.bfloat16)
                started.append(
                    send(
                        outgoing.at[t, d - 1],
                        landing.at[t, d - 1],
                        sends.at[kind, t, d - 1],
                        recvs.at[kind, t, d - 1],
                        axis,
                        d,
                    )
                )
        return started

    first_k, first_y = {}, {}

    def first_chip_sums(t):
        first_y[t] = chip_sums(
            t, "ja", nb, first_k[t], d1r, keep1, p1s, p1r, own1, y_send, y_recv, 1
        )

    spread_third(0)
    spread_second(0)
    for t in range(tiles):
        if t + 1 < tiles:
            spread_third(t + 1)
        pass_slab(t)
        if t:
            first_chip_sums(t - 1)
        first_products(t)
        first_k[t] = pair_sums(t, nb, sh1, row0, 0, d1s, d1r, keep1, 2)
        if t + 1 < tiles:
            spread_second(t + 1)
    first_chip_sums(tiles - 1)

    def gathered(t, copies, own, landing, n):
        for copy in copies:
            copy.wait_recv()
        value = own[t]
        for d in range(1, n):
            value = value + landing[t, d - 1].astype(jnp.float32)
        return value.astype(jnp.bfloat16)

    for t in range(tiles):
        fr1[:, cols(t)] = gathered(t, first_y[t], own1, p1r, nb)
    got_inv1.wait()
    new_y, new_k = {}, {}
    for t in range(tiles):
        value = jnp.dot(fr1[...], inv1[:, cols(t)], preferred_element_type=jnp.float32)
        value = value.astype(jnp.bfloat16)
        abuf[t, b, c] = value
        first_out[0, :, cols(t)] = value
        new_y[t] = [
            send(
                abuf.at[t, b, c],
                abuf.at[t, b, c],
                y_send.at[2, t, d - 1],
                y_recv.at[2, t, d - 1],
                "ja",
                d,
            )
            for d in range(1, nb)
        ]

    def spread_new(t):
        for copy in new_y[t]:
            copy.wait_recv()
        new_k[t] = [
            send(
                abuf.at[t, :, c],
                abuf.at[t, :, c],
                k_send.at[3, t, d - 1],
                k_recv.at[3, t, d - 1],
                "ka",
                d,
            )
            for d in range(1, nc)
        ]

    def second_products(t):
        for copy in new_k[t]:
            copy.wait_recv()
        masks = [chosen(row0 == q, q) for q in range(IB)]
        per = edge // sh1
        for piece in range(per):
            value = jnp.zeros((sh1, width), jnp.float32)
            for q in range(IB):
                s = q * per + piece
                rows = abuf[t, s // nc, s % nc].astype(jnp.float32)
                value = jnp.where(masks[q], rows, value)
            buse[pl.ds(piece * sh1, sh1), :] = value
        lanes = 128
        for lane in range(0, width, lanes):

            def eight(step, total):
                base = pl.multiple_of(step * 8, 8)
                rows = buse[pl.ds(base, 8), pl.ds(lane, lanes)]
                for u in range(8):
                    total = total + rows[u : u + 1] * tbuf[t, base + u, :, pl.ds(lane, lanes)].astype(
                        jnp.float32
                    )
                return total

            oacc[:, pl.ds(lane, lanes)] = lax.fori_loop(
                0, edge // 8, eight, jnp.zeros((edge, lanes), jnp.float32)
            )

    second_s, second_y = {}, {}

    def second_chip_sums(t):
        second_y[t] = chip_sums(
            t, "ia", na, second_s[t], d2r, keep2, p2s, p2r, own2, z_send, z_recv, 2
        )

    spread_new(0)
    for t in range(tiles):
        if t + 1 < tiles:
            spread_new(t + 1)
        second_products(t)
        second_s[t] = pair_sums(t, na, sh2, col0, IB, d2s, d2r, keep2, 4)
        if t:
            second_chip_sums(t - 1)
    second_chip_sums(tiles - 1)
    for t in range(tiles):
        fr2[:, cols(t)] = gathered(t, second_y[t], own2, p2r, na)
    got_inv2.wait()
    for t in range(tiles):
        value = jnp.dot(fr2[...], inv2[:, cols(t)], preferred_element_type=jnp.float32)
        second_out[0, :, cols(t)] = value.astype(jnp.bfloat16)
    for copy in sent:
        copy.wait_send()


def pair_kernel(
    sizes,
    blocks,
    places_in,
    occupied_in,
    second_in,
    third_in,
    inverse_first,
    inverse_second,
    first_out,
    second_out,
    xbuf,
    xturn,
    inv1,
    inv2,
    tz,
    ts,
    cg,
    bz,
    bs,
    br,
    pb,
    mine1,
    xs,
    xr,
    own1,
    fr1,
    sacc,
    srecv,
    own2,
    p2s,
    p2r,
    fr2,
    places,
    occupied,
    meta,
    local_sem,
    block_sem,
    meta_sems,
    tz_sems,
    far_sems,
    ts_sems,
    bz_sems,
    p1_sems,
    p2_sems,
    pair_sems,
):
    na, nb, nc = sizes
    tiles, rs, width = bs.shape
    parts, edge = tz_sems.shape[1], xbuf.shape[1]
    hr, wide = tz[0].shape[2:]
    half = edge // nc
    bf16, f32 = jnp.bfloat16, jnp.float32
    a, b, c = (lax.axis_index(name) for name in AXES)
    other = 1 - c
    sent, maybe_sent = [], []

    def send(src, dst, sems, place, **device_id):
        copy = pltpu.make_async_remote_copy(
            src_ref=src,
            dst_ref=dst,
            send_sem=sems.at[(0, *place)],
            recv_sem=sems.at[(1, *place)],
            device_id=device_id,
            device_id_type=MESH,
        )
        copy.start()
        sent.append(copy)
        return copy

    def arrival(dst, sem):
        return pltpu.make_async_remote_copy(
            src_ref=dst, dst_ref=dst, send_sem=sem, recv_sem=sem, device_id={"ka": other}, device_id_type=MESH
        )

    first, last = a == 0, a == na - 1
    inner = jnp.logical_and(a > 0, a < na - 1)
    far_piece = jnp.where(a == 1, na - 1, 0)
    far_dest = jnp.where(a == 1, 0, na - 1)

    def reaches(d):
        return jnp.logical_not(last if d == 1 else first) if d in (1, na - 1) else None

    def hears(d):
        return jnp.logical_not(first if d == 1 else last) if d in (1, na - 1) else None

    def under(condition, function):
        if condition is None:
            function()
        else:
            pl.when(condition)(function)

    def send_if(condition, src, dst, sems, place, **device_id):
        copy = pltpu.make_async_remote_copy(
            src_ref=src,
            dst_ref=dst,
            send_sem=sems.at[(0, *place)],
            recv_sem=sems.at[(1, *place)],
            device_id=device_id,
            device_id_type=MESH,
        )
        under(condition, copy.start)
        maybe_sent.append((condition, copy))

    def cols(t):
        return pl.ds(t * width, width)

    def wides(t):
        return pl.ds(t * wide, wide)

    def turn(me, d, n):
        return lax.rem(me + d, n)

    local = []

    def local_copy(src, dst):
        copy = pltpu.make_async_copy(src, dst, local_sem.at[len(local)])
        copy.start()
        local.append(copy)
        return copy

    def third_half(p, t):
        return third_in.at[0, pl.ds(pl.multiple_of(p * hr, hr), hr), wides(t)]

    barrier = pltpu.get_barrier_semaphore()
    peers = [{"ia": turn(a, d, na), "ka": turn(c, e, nc)} for d in range(na) for e in range(nc) if d or e]
    peers += [{"ja": turn(b, d, nb), "ka": turn(c, e, nc)} for d in range(1, nb) for e in range(nc)]
    for peer in peers:
        pl.semaphore_signal(barrier, inc=1, device_id=peer, device_id_type=MESH)

    got_places = local_copy(places_in, places)
    got_occupied = local_copy(occupied_in, occupied)
    own_third = [local_copy(third_half(c, t), tz[t].at[a, c]) for t in range(parts)]
    own_second = [local_copy(second_in.at[0, :, cols(t)], bz[t].at[a]) for t in range(tiles)]
    own_block = local_copy(blocks.at[0, 0, 0], xbuf.at[0])
    got_inv1 = local_copy(inverse_first, inv1)
    got_inv2 = local_copy(inverse_second, inv2)
    got_places.wait()
    got_occupied.wait()
    for slot in range(2):
        for m in range(3):
            meta[b, c, 4 * slot + m] = places[0, 0, slot, m]
        meta[b, c, 4 * slot + 3] = occupied[0, 0, slot]
    pl.semaphore_wait(barrier, len(peers))

    def third_column(t):
        for d in [*range(1, na), 0]:
            for e in range(nc):
                if d or e:
                    send_if(
                        reaches(d),
                        third_half(turn(c, e, nc), t),
                        tz[t].at[a, c],
                        tz_sems,
                        (t, d, e),
                        ia=turn(a, d, na),
                        ka=turn(c, e, nc),
                    )

    def third_near(t):
        own_third[t].wait()
        for d in [*range(1, na), 0]:
            for e in range(nc):
                if d or e:
                    under(hears(d), arrival(tz[t].at[a, c], tz_sems.at[1, t, d, e]).wait_recv)
        send_if(inner, tz[t].at[far_piece], tz[t].at[far_piece], far_sems, (0, t), ia=far_dest)

    def third_far(t):
        far = arrival(tz[t].at[na - 1], far_sems.at[1, 0, t])
        under(jnp.logical_not(inner), far.wait_recv)

    def second_column(t):
        for d in range(1, na):
            send_if(
                reaches(d),
                second_in.at[0, :, cols(t)],
                bz[t].at[a],
                bz_sems,
                (t, d - 1),
                ia=turn(a, d, na),
            )

    def second_near(t):
        own_second[t].wait()
        for d in range(1, na):
            under(hears(d), arrival(bz[t].at[a], bz_sems.at[1, t, d - 1]).wait_recv)
        send_if(inner, bz[t].at[far_piece], bz[t].at[far_piece], far_sems, (1, t), ia=far_dest)

    def second_far(t):
        far = arrival(bz[t].at[na - 1], far_sems.at[1, 1, t])
        under(jnp.logical_not(inner), far.wait_recv)

    meta_copies = [
        send(
            meta.at[b, c],
            meta.at[b, c],
            meta_sems,
            (d, e),
            ja=turn(b, d, nb),
            ka=turn(c, e, nc),
        )
        for d in range(nb)
        for e in range(nc)
        if d or e
    ]
    for t in range(parts):
        third_column(t)
    block_copy = send(blocks.at[0, 0, 1], xbuf.at[1], block_sem, (), ka=other)
    second_column(0)
    second_column(1)

    for copy in meta_copies:
        copy.wait_recv()

    def work(bb, cc):
        keep = meta[bb, cc, 3] > 0
        row, col, layer = (jnp.where(keep, meta[bb, cc, m], meta[bb, 1 - cc, 4 + m]) for m in range(3))
        return row, col, layer, jnp.where(keep, cc, 1 - cc), jnp.where(keep, 1, meta[bb, 1 - cc, 7])

    row_own, col_own, _, kept, valid_own = work(b, c)
    row_oth, col_oth, _, _, valid_oth = work(b, other)
    slot = jnp.where(kept == c, 0, 1)

    third_y = {}

    def pass_third(t):
        third_far(t)
        copies = []
        for d in range(nb):
            for e in range(nc):
                bb, cc = turn(b, d, nb), turn(c, e, nc)
                _, _, layer, span, _ = work(bb, cc)
                rows = tz[t][layer, span]
                if d or e:
                    ts[d, e, :, wides(t)] = rows
                    copies.append(
                        send(
                            ts.at[d, e, :, wides(t)],
                            cg.at[b, c, :, wides(t)],
                            ts_sems,
                            (t, d, e),
                            ja=bb,
                            ka=cc,
                        )
                    )
                else:
                    cg[b, c, :, wides(t)] = rows
        third_y[t] = copies

    ahead = [*range(2, tiles)]

    def more():
        if ahead:
            second_column(ahead.pop(0))

    for t in range(parts):
        third_near(t)
        more()
        pass_third(t)
    second_near(0)
    more()

    own_block.wait()
    block_copy.wait_recv()

    sub = 16

    def swap(step, carry):
        i0 = pl.multiple_of(step // (edge // sub) * sub, sub)
        j0 = pl.multiple_of(step % (edge // sub) * sub, sub)
        piece = xbuf[slot, pl.ds(i0, sub), pl.ds(j0, sub), :]
        xturn[pl.ds(j0, sub), pl.ds(i0, sub), :] = jnp.swapaxes(piece, 0, 1)
        return carry

    lax.fori_loop(0, (edge // sub) ** 2, swap, 0)

    def layers(t):
        return cg[:, :, :, cols(t)].reshape(edge, width)

    def halves(own, received):
        low = jnp.where(c == 0, own, received)
        high = jnp.where(c == 0, received, own)
        return jnp.concatenate([low, high], axis=0)

    def product(rows, layer_rows, pages):
        left = jnp.concatenate(pages, axis=1)
        right = jnp.concatenate([rows[u : u + 1] * layer_rows for u in range(edge)], axis=0)
        return jnp.dot(left, right, preferred_element_type=f32)

    own_rows = pl.ds(pl.multiple_of(c * half, half), half)
    other_rows = pl.ds(pl.multiple_of(other * half, half), half)

    def swap_half(t, acc, received, kind):
        return send(acc.at[t, other_rows], received.at[t], pair_sems, (kind, t), ka=other)

    def buckets(t, copy, acc, received, place_own, place_oth, me, axis, n, own, outgoing, landing, sems):
        copy.wait_recv()
        mine, theirs = acc[t, own_rows], received[t]
        copies = []
        for d in [*range(1, n), 0]:
            q = turn(me, d, n)
            value = jnp.where((place_own == q) & (valid_own > 0), mine, 0.0) + jnp.where(
                (place_oth == q) & (valid_oth > 0), theirs, 0.0
            )
            if d:
                outgoing[t, d - 1] = value.astype(bf16)
                copies.append(
                    send(outgoing.at[t, d - 1], landing.at[t, d - 1], sems, (t, d - 1), **{axis: q})
                )
            else:
                own[t] = value
        return copies

    def gathered(t, copies, own, landing, n):
        for copy in copies:
            copy.wait_recv()
        value = own[t]
        for d in range(1, n):
            value = value + landing[t, d - 1].astype(f32)
        return value.astype(bf16)

    second_k, first_y, first_k, second_s, second_y = {}, {}, {}, {}, {}
    in_plane = [work(bb, c) for bb in range(nb)]

    def pass_second(t):
        second_far(t)
        bs[t] = bz[t][col_oth]
        second_k[t] = send(bs.at[t], br.at[t], pair_sems, (0, t), ka=other)

    def first_products(t):
        second_k[t].wait_recv()
        sums = product(halves(bz[t][col_own], br[t]), layers(t), [xturn[j] for j in range(edge)])
        pb[t][b] = sums.astype(bf16)
        first_y[t] = [
            send(pb[t].at[b], pb[t].at[b], p1_sems, (t, d - 1), ja=turn(b, d, nb))
            for d in range(1, nb)
        ]

    def first_sums(t):
        for copy in first_y[t]:
            copy.wait_recv()

        def rows_of(place, rows):
            total = None
            for bb in range(nb):
                row, _, _, _, valid = in_plane[bb]
                chosen = jnp.logical_and(row == place, valid > 0)
                value = jnp.where(chosen, pb[t][bb, rows].astype(f32), 0.0)
                total = value if total is None else total + value
            return total

        xs[t, pl.ds(0, edge)] = rows_of(row_oth, pl.ds(0, edge))
        xs[t, pl.ds(edge, half)] = rows_of(b, other_rows)
        first_k[t] = send(xs.at[t], xr.at[t], pair_sems, (1, t), ka=other)
        mine1[t] = rows_of(row_own, pl.ds(0, edge))
        own1[t] = rows_of(b, own_rows)

    def first_rows(t):
        first_k[t].wait_recv()
        fr1[pl.ds(0, edge), cols(t)] = (mine1[t] + xr[t, pl.ds(0, edge)]).astype(bf16)
        fr1[pl.ds(edge, half), cols(t)] = (own1[t] + xr[t, pl.ds(edge, half)]).astype(bf16)

    pass_second(0)
    for part in range(parts):
        for copy in third_y[part]:
            copy.wait_recv()
    for t in range(tiles):
        if t + 1 < tiles:
            second_near(t + 1)
            more()
        first_products(t)
        if t + 1 < tiles:
            pass_second(t + 1)
        if t:
            first_sums(t - 1)
        if t > 1:
            first_rows(t - 2)
    first_sums(tiles - 1)
    for t in range(max(tiles - 2, 0), tiles):
        first_rows(t)
    got_inv1.wait()

    early = len(sent)

    def second_buckets(t):
        second_y[t] = buckets(
            t, second_s[t], sacc, srecv, col_own, col_oth, a, "ia", na, own2, p2s, p2r, p2_sems
        )

    for t in range(tiles):
        value = jnp.dot(fr1[...], inv1[:, cols(t)], preferred_element_type=f32).astype(bf16)
        first_out[0, :, cols(t)] = value[edge:]
        sacc[t] = product(value[:edge], layers(t), [xbuf[slot, i] for i in range(edge)])
        second_s[t] = swap_half(t, sacc, srecv, 2)
        if t:
            second_buckets(t - 1)
    second_buckets(tiles - 1)
    for copy in sent[:early]:
        copy.wait_send()
    for condition, copy in maybe_sent:
        under(condition, copy.wait_send)
    for t in range(tiles):
        fr2[:, cols(t)] = gathered(t, second_y[t], own2, p2r, na)
    got_inv2.wait()
    for t in range(tiles):
        value = jnp.dot(fr2[...], inv2[:, cols(t)], preferred_element_type=f32)
        second_out[0, :, cols(t)] = value.astype(bf16)
    for copy in sent[early:]:
        copy.wait_send()


def pair_call(sizes, blocks, coordinates, occupancy, second_factor, third_factor, inverse_first, inverse_second):
    na, nb, nc = sizes
    edge, rank = blocks.shape[-1], inverse_first.shape[0]
    tiles, parts = PAIR_TILES, PARTS
    width = rank // tiles
    rs, hr = second_factor.shape[1], third_factor.shape[1] // nc
    half = edge // nc
    bf16, f32 = jnp.bfloat16, jnp.float32
    dma = pltpu.SemaphoreType.DMA
    vmem = pl.BlockSpec(memory_space=pltpu.VMEM)
    anywhere = pl.BlockSpec(memory_space=pl.ANY)
    places = jnp.transpose(coordinates, (1, 2, 3, 0))

    def sums(n):
        return [
            pltpu.VMEM((tiles, half, width), f32),
            pltpu.VMEM((tiles, n - 1, half, width), bf16),
            pltpu.VMEM((tiles, n - 1, half, width), bf16),
            pltpu.VMEM((half, rank), bf16),
        ]

    def swapped():
        return [pltpu.VMEM((tiles, edge, width), f32), pltpu.VMEM((tiles, half, width), f32)]

    def one_half():
        return [pltpu.VMEM((tiles, half, width), bf16)] * 2

    scratch = [
        pltpu.VMEM((2, edge, edge, edge), bf16),
        pltpu.VMEM((edge, edge, edge), bf16),
        pltpu.VMEM((rank, rank), bf16),
        pltpu.VMEM((rank, rank), bf16),
        (pltpu.VMEM((na, nc, hr, rank // parts), bf16),) * parts,
        pltpu.VMEM((nb, nc, hr, rank), bf16),
        pltpu.VMEM((nb, nc, hr, rank), bf16),
        (pltpu.VMEM((na, rs, width), bf16),) * tiles,
        *one_half(),
        (pltpu.VMEM((nb, edge, width), bf16),) * tiles,
        pltpu.VMEM((tiles, edge, width), f32),
        pltpu.VMEM((tiles, edge + half, width), f32),
        pltpu.VMEM((tiles, edge + half, width), f32),
        pltpu.VMEM((tiles, half, width), f32),
        pltpu.VMEM((edge + half, rank), bf16),
        *swapped(),
        *sums(na),
        pltpu.SMEM(places.shape, jnp.int32),
        pltpu.SMEM(occupancy.shape, jnp.int32),
        pltpu.SMEM((nb, nc, 8), jnp.int32),
        dma((parts + tiles + 5,)),
        dma((2,)),
        dma((2, nb, nc)),
        dma((2, parts, na, nc)),
        dma((2, 2, max(parts, tiles))),
        dma((2, parts, nb, nc)),
        dma((2, tiles, na - 1)),
        dma((2, tiles, nb - 1)),
        dma((2, tiles, na - 1)),
        dma((2, 3, tiles)),
    ]
    return pl.pallas_call(
        functools.partial(pair_kernel, sizes),
        name="als_pair",
        out_shape=(
            jax.ShapeDtypeStruct((1, half, rank), bf16),
            jax.ShapeDtypeStruct((1, half, rank), bf16),
        ),
        in_specs=[anywhere, anywhere, anywhere, vmem, vmem, anywhere, anywhere],
        out_specs=(vmem, vmem),
        scratch_shapes=scratch,
        compiler_params=pltpu.CompilerParams(
            collective_id=0, has_side_effects=True, vmem_limit_bytes=VMEM_LIMIT
        ),
    )(blocks, places, occupancy, second_factor, third_factor, inverse_first, inverse_second)


def pairs_fit(sizes, blocks, second_factor, third_factor):
    na, nb, nc = sizes
    edge = blocks.shape[-1]
    third_rows = third_factor.shape[1]
    return (
        nc == 2
        and na == JB
        and nb == IB
        and second_factor.shape[1] * nc == edge
        and third_rows * nb == edge
        and third_rows % (16 * nc) == 0
    )


def general_call(
    sizes,
    blocks,
    coordinates,
    occupancy,
    second_factor,
    third_factor,
    inverse_first,
    inverse_second,
):
    na, nb, nc = sizes
    edge, rank = blocks.shape[-1], inverse_first.shape[0]
    tiles = TILES
    width = rank // tiles
    rs, rt = second_factor.shape[1], third_factor.shape[1]
    sh1, sh2 = IB * edge // (nb * nc), JB * edge // (na * nc)
    bf16, f32 = jnp.bfloat16, jnp.float32
    dma = pltpu.SemaphoreType.DMA
    widest_k = max(nc - 1, 1)
    vmem = pl.BlockSpec(memory_space=pltpu.VMEM)
    anywhere = pl.BlockSpec(memory_space=pl.ANY)
    scratch = [
        pltpu.VMEM((2, edge, edge, edge), bf16),
        pltpu.VMEM((rank, rank), bf16),
        pltpu.VMEM((rank, rank), bf16),
        pltpu.VMEM((IB + JB, width), f32),
        pltpu.VMEM((IB + JB, width), f32),
        pltpu.VMEM((tiles, na, nb, rt, width), bf16),
        pltpu.VMEM((tiles, na, nc, rs, width), bf16),
        pltpu.VMEM((tiles, edge, width), bf16),
        pltpu.VMEM((tiles, edge, width), bf16),
        pltpu.VMEM((edge, width), bf16),
        pltpu.VMEM((edge, width), f32),
        pltpu.VMEM((tiles, edge, edge, width), bf16),
        pltpu.VMEM((edge, width), f32),
        pltpu.VMEM((tiles, nc - 1, nb, sh1, width), bf16),
        pltpu.VMEM((tiles, nc - 1, nb, sh1, width), bf16),
        pltpu.VMEM((tiles, nb, sh1, width), f32),
        pltpu.VMEM((tiles, nb - 1, sh1, width), bf16),
        pltpu.VMEM((tiles, nb - 1, sh1, width), bf16),
        pltpu.VMEM((tiles, sh1, width), f32),
        pltpu.VMEM((sh1, rank), bf16),
        pltpu.VMEM((tiles, nb, nc, sh1, width), bf16),
        pltpu.VMEM((tiles, nc - 1, na, sh2, width), bf16),
        pltpu.VMEM((tiles, nc - 1, na, sh2, width), bf16),
        pltpu.VMEM((tiles, na, sh2, width), f32),
        pltpu.VMEM((tiles, na - 1, sh2, width), bf16),
        pltpu.VMEM((tiles, na - 1, sh2, width), bf16),
        pltpu.VMEM((tiles, sh2, width), f32),
        pltpu.VMEM((sh2, rank), bf16),
        pltpu.SMEM(coordinates.shape, jnp.int32),
        pltpu.SMEM(occupancy.shape, jnp.int32),
        dma((2 * tiles + 5,)),
        dma((2,)),
        dma((2,)),
        dma((3, tiles, na - 1)),
        dma((3, tiles, na - 1)),
        dma((3, tiles, nb - 1)),
        dma((3, tiles, nb - 1)),
        dma((5, tiles, widest_k)),
        dma((5, tiles, widest_k)),
    ]
    return pl.pallas_call(
        functools.partial(kernel, sizes),
        name="als",
        out_shape=(
            jax.ShapeDtypeStruct((1, sh1, rank), bf16),
            jax.ShapeDtypeStruct((1, sh2, rank), bf16),
        ),
        in_specs=[anywhere, anywhere, anywhere, vmem, vmem, anywhere, anywhere],
        out_specs=(vmem, vmem),
        scratch_shapes=scratch,
        compiler_params=pltpu.CompilerParams(
            collective_id=0, has_side_effects=True, vmem_limit_bytes=67043328
        ),
    )(blocks, coordinates, occupancy, second_factor, third_factor, inverse_first, inverse_second)


def body(sizes, *args):
    blocks, second_factor, third_factor = args[0], args[3], args[4]
    vmem = pl.BlockSpec(memory_space=pltpu.VMEM)
    call = pair_call if pairs_fit(sizes, blocks, second_factor, third_factor) else general_call
    results = call(sizes, *args)
    return pl.pallas_call(
        hand_over,
        name="hand_over",
        out_shape=tuple(jax.ShapeDtypeStruct(x.shape, x.dtype) for x in results),
        in_specs=[vmem, vmem],
        out_specs=(vmem, vmem),
    )(*results)


def hand_over(first_in, second_in, first_out, second_out):
    first_out[...] = first_in[...]
    second_out[...] = second_in[...]


def solution(mesh):
    sizes = tuple(mesh.shape[name] for name in AXES)
    in_specs = (
        P("ia", "ja", "ka", None, None, None),
        P(None, "ia", "ja", "ka"),
        P("ia", "ja", "ka"),
        P("ja", ("ia", "ka"), None),
        P("ka", ("ia", "ja"), None),
        P(),
        P(),
    )
    out_specs = (P("ia", ("ja", "ka"), None), P("ja", ("ia", "ka"), None))
    return jax.shard_map(
        functools.partial(body, sizes),
        mesh=mesh,
        in_specs=in_specs,
        out_specs=out_specs,
        check_vma=False,
    )
```

```python
import functools

import jax
import jax.numpy as jnp
from jax import lax
from jax.experimental import pallas as pl
from jax.experimental.pallas import tpu as pltpu
from jax.sharding import PartitionSpec as P

IB = 4
JB = 4
TILES = 4
PAIR_TILES = 2
PARTS = 1
VMEM_LIMIT = 67043328
MESH = pl.DeviceIdType.MESH
AXES = ("ia", "ja", "ka")


def kernel(
    sizes,
    blocks,
    places_in,
    occupied_in,
    second_in,
    third_in,
    inverse_first,
    inverse_second,
    first_out,
    second_out,
    xbuf,
    inv1,
    inv2,
    meta_s,
    meta_r,
    cbuf,
    bbuf,
    slab_s,
    slab_r,
    cuse,
    buse,
    tbuf,
    oacc,
    d1s,
    d1r,
    keep1,
    p1s,
    p1r,
    own1,
    fr1,
    abuf,
    d2s,
    d2r,
    keep2,
    p2s,
    p2r,
    own2,
    fr2,
    places,
    occupied,
    local_sem,
    once_send,
    once_recv,
    z_send,
    z_recv,
    y_send,
    y_recv,
    k_send,
    k_recv,
):
    na, nb, nc = sizes
    tiles, edge, width = slab_s.shape
    rs, rt = bbuf.shape[3], cbuf.shape[3]
    sh1, sh2 = abuf.shape[3], own2.shape[1]
    a, b, c = (lax.axis_index(name) for name in AXES)
    sent = []

    def away(axis, d):
        n = sizes[AXES.index(axis)]
        me = (a, b, c)[AXES.index(axis)]
        return lax.rem(me + d, n)

    def send(src, dst, send_sem, recv_sem, axis, d):
        copy = pltpu.make_async_remote_copy(
            src_ref=src,
            dst_ref=dst,
            send_sem=send_sem,
            recv_sem=recv_sem,
            device_id={axis: away(axis, d)},
            device_id_type=MESH,
        )
        copy.start()
        sent.append(copy)
        return copy

    def cols(t):
        return pl.ds(t * width, width)

    local = []

    def local_copy(src, dst):
        copy = pltpu.make_async_copy(src, dst, local_sem.at[len(local)])
        copy.start()
        local.append(copy)
        return copy

    got_places = local_copy(places_in, places)
    got_occupied = local_copy(occupied_in, occupied)
    own_third = [
        local_copy(third_in.at[0, :, cols(t)], cbuf.at[t, a, b]) for t in range(tiles)
    ]
    own_second = [
        local_copy(second_in.at[0, :, cols(t)], bbuf.at[t, a, c]) for t in range(tiles)
    ]
    own_block = local_copy(blocks.at[0, 0, 0], xbuf.at[0])
    got_inv1 = local_copy(inverse_first, inv1)
    got_inv2 = local_copy(inverse_second, inv2)

    barrier = pltpu.get_barrier_semaphore()
    for axis, n in zip(AXES, sizes):
        for d in range(1, n):
            pl.semaphore_signal(
                barrier, inc=1, device_id={axis: away(axis, d)}, device_id_type=MESH
            )
    got_places.wait()
    got_occupied.wait()
    keep = occupied[0, 0, 0] > 0
    row0, col0, layer0 = (places[m, 0, 0, 0] for m in range(3))
    row1, col1, layer1 = (places[m, 0, 0, 1] for m in range(3))
    weight1 = jnp.where(occupied[0, 0, 1] > 0, 1.0, 0.0).astype(jnp.float32)
    for q in range(IB):
        value = jnp.where(row1 == q, weight1, 0.0)
        meta_s[pl.ds(q, 1), :] = jnp.full((1, width), value, jnp.float32)
    for q in range(JB):
        value = jnp.where(col1 == q, weight1, 0.0)
        meta_s[pl.ds(IB + q, 1), :] = jnp.full((1, width), value, jnp.float32)
    pl.semaphore_wait(barrier, (na - 1) + (nb - 1) + (nc - 1))

    def chosen(own_value, row):
        own = jnp.where(own_value, 1.0, 0.0).astype(jnp.float32)
        return jnp.where(keep, jnp.full((1, width), own, jnp.float32), meta_r[pl.ds(row, 1), :]) > 0.5

    def third_column(t):
        return [
            send(
                third_in.at[0, :, cols(t)],
                cbuf.at[t, a, b],
                z_send.at[0, t, d - 1],
                z_recv.at[0, t, d - 1],
                "ia",
                d,
            )
            for d in range(1, na)
        ]

    def second_column(t):
        return [
            send(
                second_in.at[0, :, cols(t)],
                bbuf.at[t, a, c],
                z_send.at[1, t, d - 1],
                z_recv.at[1, t, d - 1],
                "ia",
                d,
            )
            for d in range(1, na)
        ]

    third_z, second_z = {}, {}
    third_z[0] = third_column(0)
    block_copy = send(blocks.at[0, 0, 1], xbuf.at[1], once_send.at[0], once_recv.at[0], "ka", 1)
    meta_copy = send(meta_s, meta_r, once_send.at[1], once_recv.at[1], "ka", 1)
    for t in range(1, tiles):
        third_z[t] = third_column(t)
        second_z[t - 1] = second_column(t - 1)
    second_z[tiles - 1] = second_column(tiles - 1)

    third_y, second_k, slab_copy = {}, {}, {}

    def spread_third(t):
        own_third[t].wait()
        for copy in third_z[t]:
            copy.wait_recv()
        third_y[t] = [
            send(
                cbuf.at[t, :, b],
                cbuf.at[t, :, b],
                y_send.at[0, t, d - 1],
                y_recv.at[0, t, d - 1],
                "ja",
                d,
            )
            for d in range(1, nb)
        ]

    def spread_second(t):
        own_second[t].wait()
        for copy in second_z[t]:
            copy.wait_recv()
        second_k[t] = [
            send(
                bbuf.at[t, :, c],
                bbuf.at[t, :, c],
                k_send.at[0, t, d - 1],
                k_recv.at[0, t, d - 1],
                "ka",
                d,
            )
            for d in range(1, nc)
        ]

    def layer_piece(t, layer, piece):
        per = edge // rt
        total = na * nb * rt // edge
        value = None
        for q in range(total):
            s = q * per + piece
            rows = cbuf[t, s // nb, s % nb]
            value = rows if value is None else jnp.where(layer == q, rows, value)
        return value

    def pass_slab(t):
        for copy in third_y[t]:
            copy.wait_recv()
        for piece in range(edge // rt):
            slab_s[t, pl.ds(piece * rt, rt), :] = layer_piece(t, layer1, piece)
        slab_copy[t] = send(
            slab_s.at[t], slab_r.at[t], k_send.at[1, t, 0], k_recv.at[1, t, 0], "ka", 1
        )
        for piece in range(edge // rt):
            cuse[pl.ds(piece * rt, rt), :] = layer_piece(t, layer0, piece)

    def first_products(t):
        for copy in second_k[t]:
            copy.wait_recv()
        if t == 0:
            own_block.wait()
            block_copy.wait_recv()
            meta_copy.wait_recv()
        masks = [chosen(col0 == q, IB + q) for q in range(JB)]
        per = edge // rs
        for piece in range(per):
            value = jnp.zeros((rs, width), jnp.float32)
            for q in range(JB):
                s = q * per + piece
                rows = bbuf[t, s // nc, s % nc].astype(jnp.float32)
                value = jnp.where(masks[q], rows, value)
            buse[pl.ds(piece * rs, rs), :] = value
        slab_copy[t].wait_recv()
        cuse[...] = jnp.where(keep, cuse[...], slab_r[t])
        slot = jnp.where(keep, 0, 1)

        def eight(step, carry):
            base = pl.multiple_of(step * 8, 8)
            sums = []
            for u in range(8):
                product = jnp.dot(
                    xbuf[slot, base + u], cuse[...], preferred_element_type=jnp.float32
                )
                tbuf[t, base + u] = product.astype(jnp.bfloat16)
                sums.append(jnp.sum(product * buse[...], axis=0, keepdims=True))
            oacc[pl.ds(base, 8), :] = jnp.concatenate(sums, axis=0)
            return carry

        lax.fori_loop(0, edge // 8, eight, 0)

    def owned_piece(owner, rows, own_place, meta_row):
        start = owner * rows
        block = start // edge
        off = pl.multiple_of(start % edge, rows)
        mask = chosen(own_place == block, meta_row + block)
        return jnp.where(mask, oacc[pl.ds(off, rows), :], 0.0)

    def pair_sums(t, n, rows, own_place, meta_row, outgoing, arriving, kept, kind):
        copies = []
        for d in range(1, nc):
            for m in range(n):
                owner = m * nc + away("ka", d)
                outgoing[t, d - 1, m] = owned_piece(owner, rows, own_place, meta_row).astype(
                    jnp.bfloat16
                )
            copies.append(
                send(
                    outgoing.at[t, d - 1],
                    arriving.at[t, d - 1],
                    k_send.at[kind, t, d - 1],
                    k_recv.at[kind, t, d - 1],
                    "ka",
                    d,
                )
            )
        for m in range(n):
            kept[t, m] = owned_piece(m * nc + c, rows, own_place, meta_row)
        return copies

    def chip_sums(t, axis, n, copies, arriving, kept, outgoing, landing, own, sends, recvs, kind):
        for copy in copies:
            copy.wait_recv()
        started = []
        for d in range(n):
            m = away(axis, d)
            value = kept[t, m]
            for e in range(1, nc):
                value = value + arriving[t, e - 1, m].astype(jnp.float32)
            if d == 0:
                own[t] = value
            else:
                outgoing[t, d - 1] = value.astype(jnp.bfloat16)
                started.append(
                    send(
                        outgoing.at[t, d - 1],
                        landing.at[t, d - 1],
                        sends.at[kind, t, d - 1],
                        recvs.at[kind, t, d - 1],
                        axis,
                        d,
                    )
                )
        return started

    first_k, first_y = {}, {}

    def first_chip_sums(t):
        first_y[t] = chip_sums(
            t, "ja", nb, first_k[t], d1r, keep1, p1s, p1r, own1, y_send, y_recv, 1
        )

    spread_third(0)
    spread_second(0)
    for t in range(tiles):
        if t + 1 < tiles:
            spread_third(t + 1)
        pass_slab(t)
        if t:
            first_chip_sums(t - 1)
        first_products(t)
        first_k[t] = pair_sums(t, nb, sh1, row0, 0, d1s, d1r, keep1, 2)
        if t + 1 < tiles:
            spread_second(t + 1)
    first_chip_sums(tiles - 1)

    def gathered(t, copies, own, landing, n):
        for copy in copies:
            copy.wait_recv()
        value = own[t]
        for d in range(1, n):
            value = value + landing[t, d - 1].astype(jnp.float32)
        return value.astype(jnp.bfloat16)

    for t in range(tiles):
        fr1[:, cols(t)] = gathered(t, first_y[t], own1, p1r, nb)
    got_inv1.wait()
    new_y, new_k = {}, {}
    for t in range(tiles):
        value = jnp.dot(fr1[...], inv1[:, cols(t)], preferred_element_type=jnp.float32)
        value = value.astype(jnp.bfloat16)
        abuf[t, b, c] = value
        first_out[0, :, cols(t)] = value
        new_y[t] = [
            send(
                abuf.at[t, b, c],
                abuf.at[t, b, c],
                y_send.at[2, t, d - 1],
                y_recv.at[2, t, d - 1],
                "ja",
                d,
            )
            for d in range(1, nb)
        ]

    def spread_new(t):
        for copy in new_y[t]:
            copy.wait_recv()
        new_k[t] = [
            send(
                abuf.at[t, :, c],
                abuf.at[t, :, c],
                k_send.at[3, t, d - 1],
                k_recv.at[3, t, d - 1],
                "ka",
                d,
            )
            for d in range(1, nc)
        ]

    def second_products(t):
        for copy in new_k[t]:
            copy.wait_recv()
        masks = [chosen(row0 == q, q) for q in range(IB)]
        per = edge // sh1
        for piece in range(per):
            value = jnp.zeros((sh1, width), jnp.float32)
            for q in range(IB):
                s = q * per + piece
                rows = abuf[t, s // nc, s % nc].astype(jnp.float32)
                value = jnp.where(masks[q], rows, value)
            buse[pl.ds(piece * sh1, sh1), :] = value
        lanes = 128
        for lane in range(0, width, lanes):

            def eight(step, total):
                base = pl.multiple_of(step * 8, 8)
                rows = buse[pl.ds(base, 8), pl.ds(lane, lanes)]
                for u in range(8):
                    total = total + rows[u : u + 1] * tbuf[t, base + u, :, pl.ds(lane, lanes)].astype(
                        jnp.float32
                    )
                return total

            oacc[:, pl.ds(lane, lanes)] = lax.fori_loop(
                0, edge // 8, eight, jnp.zeros((edge, lanes), jnp.float32)
            )

    second_s, second_y = {}, {}

    def second_chip_sums(t):
        second_y[t] = chip_sums(
            t, "ia", na, second_s[t], d2r, keep2, p2s, p2r, own2, z_send, z_recv, 2
        )

    spread_new(0)
    for t in range(tiles):
        if t + 1 < tiles:
            spread_new(t + 1)
        second_products(t)
        second_s[t] = pair_sums(t, na, sh2, col0, IB, d2s, d2r, keep2, 4)
        if t:
            second_chip_sums(t - 1)
    second_chip_sums(tiles - 1)
    for t in range(tiles):
        fr2[:, cols(t)] = gathered(t, second_y[t], own2, p2r, na)
    got_inv2.wait()
    for t in range(tiles):
        value = jnp.dot(fr2[...], inv2[:, cols(t)], preferred_element_type=jnp.float32)
        second_out[0, :, cols(t)] = value.astype(jnp.bfloat16)
    for copy in sent:
        copy.wait_send()


def pair_kernel(
    sizes,
    blocks,
    places_in,
    occupied_in,
    second_in,
    third_in,
    inverse_first,
    inverse_second,
    first_out,
    second_out,
    xbuf,
    xturn,
    inv1,
    inv2,
    tz,
    ts,
    cg,
    bz,
    bs,
    br,
    pb,
    mine1,
    xs,
    xr,
    own1,
    fr1,
    sacc,
    srecv,
    own2,
    p2s,
    p2r,
    fr2,
    places,
    occupied,
    meta,
    local_sem,
    block_sem,
    meta_sems,
    tz_sems,
    far_sems,
    ts_sems,
    bz_sems,
    p1_sems,
    p2_sems,
    pair_sems,
):
    na, nb, nc = sizes
    tiles, rs, width = bs.shape
    parts, edge = tz_sems.shape[1], xbuf.shape[1]
    hr, wide = tz[0].shape[2:]
    half = edge // nc
    bf16, f32 = jnp.bfloat16, jnp.float32
    a, b, c = (lax.axis_index(name) for name in AXES)
    other = 1 - c
    sent, maybe_sent = [], []

    def send(src, dst, sems, place, **device_id):
        copy = pltpu.make_async_remote_copy(
            src_ref=src,
            dst_ref=dst,
            send_sem=sems.at[(0, *place)],
            recv_sem=sems.at[(1, *place)],
            device_id=device_id,
            device_id_type=MESH,
        )
        copy.start()
        sent.append(copy)
        return copy

    def arrival(dst, sem):
        return pltpu.make_async_remote_copy(
            src_ref=dst, dst_ref=dst, send_sem=sem, recv_sem=sem, device_id={"ka": other}, device_id_type=MESH
        )

    first, last = a == 0, a == na - 1
    inner = jnp.logical_and(a > 0, a < na - 1)
    far_piece = jnp.where(a == 1, na - 1, 0)
    far_dest = jnp.where(a == 1, 0, na - 1)

    def reaches(d):
        return jnp.logical_not(last if d == 1 else first) if d in (1, na - 1) else None

    def hears(d):
        return jnp.logical_not(first if d == 1 else last) if d in (1, na - 1) else None

    def under(condition, function):
        if condition is None:
            function()
        else:
            pl.when(condition)(function)

    def send_if(condition, src, dst, sems, place, **device_id):
        copy = pltpu.make_async_remote_copy(
            src_ref=src,
            dst_ref=dst,
            send_sem=sems.at[(0, *place)],
            recv_sem=sems.at[(1, *place)],
            device_id=device_id,
            device_id_type=MESH,
        )
        under(condition, copy.start)
        maybe_sent.append((condition, copy))

    def cols(t):
        return pl.ds(t * width, width)

    def wides(t):
        return pl.ds(t * wide, wide)

    def turn(me, d, n):
        return lax.rem(me + d, n)

    local = []

    def local_copy(src, dst):
        copy = pltpu.make_async_copy(src, dst, local_sem.at[len(local)])
        copy.start()
        local.append(copy)
        return copy

    def third_half(p, t):
        return third_in.at[0, pl.ds(pl.multiple_of(p * hr, hr), hr), wides(t)]

    barrier = pltpu.get_barrier_semaphore()
    peers = [{"ia": turn(a, d, na), "ka": turn(c, e, nc)} for d in range(na) for e in range(nc) if d or e]
    peers += [{"ja": turn(b, d, nb), "ka": turn(c, e, nc)} for d in range(1, nb) for e in range(nc)]
    for peer in peers:
        pl.semaphore_signal(barrier, inc=1, device_id=peer, device_id_type=MESH)

    got_places = local_copy(places_in, places)
    got_occupied = local_copy(occupied_in, occupied)
    own_third = [local_copy(third_half(c, t), tz[t].at[a, c]) for t in range(parts)]
    own_second = [local_copy(second_in.at[0, :, cols(t)], bz[t].at[a]) for t in range(tiles)]
    own_block = local_copy(blocks.at[0, 0, 0], xbuf.at[0])
    got_inv1 = local_copy(inverse_first, inv1)
    got_inv2 = local_copy(inverse_second, inv2)
    got_places.wait()
    got_occupied.wait()
    for slot in range(2):
        for m in range(3):
            meta[b, c, 4 * slot + m] = places[0, 0, slot, m]
        meta[b, c, 4 * slot + 3] = occupied[0, 0, slot]
    pl.semaphore_wait(barrier, len(peers))

    def third_column(t):
        for d in [*range(1, na), 0]:
            for e in range(nc):
                if d or e:
                    send_if(
                        reaches(d),
                        third_half(turn(c, e, nc), t),
                        tz[t].at[a, c],
                        tz_sems,
                        (t, d, e),
                        ia=turn(a, d, na),
                        ka=turn(c, e, nc),
                    )

    def third_near(t):
        own_third[t].wait()
        for d in [*range(1, na), 0]:
            for e in range(nc):
                if d or e:
                    under(hears(d), arrival(tz[t].at[a, c], tz_sems.at[1, t, d, e]).wait_recv)
        send_if(inner, tz[t].at[far_piece], tz[t].at[far_piece], far_sems, (0, t), ia=far_dest)

    def third_far(t):
        far = arrival(tz[t].at[na - 1], far_sems.at[1, 0, t])
        under(jnp.logical_not(inner), far.wait_recv)

    def second_column(t):
        for d in range(1, na):
            send_if(
                reaches(d),
                second_in.at[0, :, cols(t)],
                bz[t].at[a],
                bz_sems,
                (t, d - 1),
                ia=turn(a, d, na),
            )

    def second_near(t):
        own_second[t].wait()
        for d in range(1, na):
            under(hears(d), arrival(bz[t].at[a], bz_sems.at[1, t, d - 1]).wait_recv)
        send_if(inner, bz[t].at[far_piece], bz[t].at[far_piece], far_sems, (1, t), ia=far_dest)

    def second_far(t):
        far = arrival(bz[t].at[na - 1], far_sems.at[1, 1, t])
        under(jnp.logical_not(inner), far.wait_recv)

    for t in range(parts):
        third_column(t)
    meta_copies = [
        send(
            meta.at[b, c],
            meta.at[b, c],
            meta_sems,
            (d, e),
            ja=turn(b, d, nb),
            ka=turn(c, e, nc),
        )
        for d in range(nb)
        for e in range(nc)
        if d or e
    ]
    block_copy = send(blocks.at[0, 0, 1], xbuf.at[1], block_sem, (), ka=other)
    second_column(0)

    for copy in meta_copies:
        copy.wait_recv()

    def work(bb, cc):
        keep = meta[bb, cc, 3] > 0
        row, col, layer = (jnp.where(keep, meta[bb, cc, m], meta[bb, 1 - cc, 4 + m]) for m in range(3))
        return row, col, layer, jnp.where(keep, cc, 1 - cc), jnp.where(keep, 1, meta[bb, 1 - cc, 7])

    row_own, col_own, _, kept, valid_own = work(b, c)
    row_oth, col_oth, _, _, valid_oth = work(b, other)
    slot = jnp.where(kept == c, 0, 1)

    third_y = {}

    def pass_third(t):
        third_far(t)
        copies = []
        for d in range(nb):
            for e in range(nc):
                bb, cc = turn(b, d, nb), turn(c, e, nc)
                _, _, layer, span, _ = work(bb, cc)
                rows = tz[t][layer, span]
                if d or e:
                    ts[d, e, :, wides(t)] = rows
                    copies.append(
                        send(
                            ts.at[d, e, :, wides(t)],
                            cg.at[b, c, :, wides(t)],
                            ts_sems,
                            (t, d, e),
                            ja=bb,
                            ka=cc,
                        )
                    )
                else:
                    cg[b, c, :, wides(t)] = rows
        third_y[t] = copies

    ahead = [*range(1, tiles)]

    def more():
        if ahead:
            second_column(ahead.pop(0))

    for t in range(parts):
        third_near(t)
        more()
        pass_third(t)
    second_near(0)
    more()

    own_block.wait()
    block_copy.wait_recv()

    sub = 16

    def swap(step, carry):
        i0 = pl.multiple_of(step // (edge // sub) * sub, sub)
        j0 = pl.multiple_of(step % (edge // sub) * sub, sub)
        piece = xbuf[slot, pl.ds(i0, sub), pl.ds(j0, sub), :]
        xturn[pl.ds(j0, sub), pl.ds(i0, sub), :] = jnp.swapaxes(piece, 0, 1)
        return carry

    lax.fori_loop(0, (edge // sub) ** 2, swap, 0)

    def layers(t):
        return cg[:, :, :, cols(t)].reshape(edge, width)

    def halves(own, received):
        low = jnp.where(c == 0, own, received)
        high = jnp.where(c == 0, received, own)
        return jnp.concatenate([low, high], axis=0)

    def product(rows, layer_rows, pages):
        left = jnp.concatenate(pages, axis=1)
        right = jnp.concatenate([rows[u : u + 1] * layer_rows for u in range(edge)], axis=0)
        return jnp.dot(left, right, preferred_element_type=f32)

    own_rows = pl.ds(pl.multiple_of(c * half, half), half)
    other_rows = pl.ds(pl.multiple_of(other * half, half), half)

    def swap_half(t, acc, received, kind):
        return send(acc.at[t, other_rows], received.at[t], pair_sems, (kind, t), ka=other)

    def buckets(t, copy, acc, received, place_own, place_oth, me, axis, n, own, outgoing, landing, sems):
        copy.wait_recv()
        mine, theirs = acc[t, own_rows], received[t]
        copies = []
        for d in [*range(1, n), 0]:
            q = turn(me, d, n)
            value = jnp.where((place_own == q) & (valid_own > 0), mine, 0.0) + jnp.where(
                (place_oth == q) & (valid_oth > 0), theirs, 0.0
            )
            if d:
                outgoing[t, d - 1] = value.astype(bf16)
                copies.append(
                    send(outgoing.at[t, d - 1], landing.at[t, d - 1], sems, (t, d - 1), **{axis: q})
                )
            else:
                own[t] = value
        return copies

    def gathered(t, copies, own, landing, n):
        for copy in copies:
            copy.wait_recv()
        value = own[t]
        for d in range(1, n):
            value = value + landing[t, d - 1].astype(f32)
        return value.astype(bf16)

    second_k, first_y, first_k, second_s, second_y = {}, {}, {}, {}, {}
    in_plane = [work(bb, c) for bb in range(nb)]

    def pass_second(t):
        second_far(t)
        bs[t] = bz[t][col_oth]
        second_k[t] = send(bs.at[t], br.at[t], pair_sems, (0, t), ka=other)

    def first_products(t):
        second_k[t].wait_recv()
        sums = product(halves(bz[t][col_own], br[t]), layers(t), [xturn[j] for j in range(edge)])
        pb[t][b] = sums.astype(bf16)
        first_y[t] = [
            send(pb[t].at[b], pb[t].at[b], p1_sems, (t, d - 1), ja=turn(b, d, nb))
            for d in range(1, nb)
        ]

    def first_sums(t):
        for copy in first_y[t]:
            copy.wait_recv()

        def rows_of(place, rows):
            total = None
            for bb in range(nb):
                row, _, _, _, valid = in_plane[bb]
                chosen = jnp.logical_and(row == place, valid > 0)
                value = jnp.where(chosen, pb[t][bb, rows].astype(f32), 0.0)
                total = value if total is None else total + value
            return total

        xs[t, pl.ds(0, edge)] = rows_of(row_oth, pl.ds(0, edge))
        xs[t, pl.ds(edge, half)] = rows_of(b, other_rows)
        first_k[t] = send(xs.at[t], xr.at[t], pair_sems, (1, t), ka=other)
        mine1[t] = rows_of(row_own, pl.ds(0, edge))
        own1[t] = rows_of(b, own_rows)

    def first_rows(t):
        first_k[t].wait_recv()
        fr1[pl.ds(0, edge), cols(t)] = (mine1[t] + xr[t, pl.ds(0, edge)]).astype(bf16)
        fr1[pl.ds(edge, half), cols(t)] = (own1[t] + xr[t, pl.ds(edge, half)]).astype(bf16)

    pass_second(0)
    for part in range(parts):
        for copy in third_y[part]:
            copy.wait_recv()
    for t in range(tiles):
        if t + 1 < tiles:
            second_near(t + 1)
            more()
        first_products(t)
        if t + 1 < tiles:
            pass_second(t + 1)
        if t:
            first_sums(t - 1)
        if t > 1:
            first_rows(t - 2)
    first_sums(tiles - 1)
    for t in range(max(tiles - 2, 0), tiles):
        first_rows(t)
    got_inv1.wait()

    early = len(sent)

    def second_buckets(t):
        second_y[t] = buckets(
            t, second_s[t], sacc, srecv, col_own, col_oth, a, "ia", na, own2, p2s, p2r, p2_sems
        )

    for t in range(tiles):
        value = jnp.dot(fr1[...], inv1[:, cols(t)], preferred_element_type=f32).astype(bf16)
        first_out[0, :, cols(t)] = value[edge:]
        if t:
            second_buckets(t - 1)
        sacc[t] = product(value[:edge], layers(t), [xbuf[slot, i] for i in range(edge)])
        second_s[t] = swap_half(t, sacc, srecv, 2)
    second_buckets(tiles - 1)
    for copy in sent[:early]:
        copy.wait_send()
    for condition, copy in maybe_sent:
        under(condition, copy.wait_send)
    for t in range(tiles):
        fr2[:, cols(t)] = gathered(t, second_y[t], own2, p2r, na)
    got_inv2.wait()
    for t in range(tiles):
        value = jnp.dot(fr2[...], inv2[:, cols(t)], preferred_element_type=f32)
        second_out[0, :, cols(t)] = value.astype(bf16)
    for copy in sent[early:]:
        copy.wait_send()


def pair_call(sizes, blocks, coordinates, occupancy, second_factor, third_factor, inverse_first, inverse_second):
    na, nb, nc = sizes
    edge, rank = blocks.shape[-1], inverse_first.shape[0]
    tiles, parts = PAIR_TILES, PARTS
    width = rank // tiles
    rs, hr = second_factor.shape[1], third_factor.shape[1] // nc
    half = edge // nc
    bf16, f32 = jnp.bfloat16, jnp.float32
    dma = pltpu.SemaphoreType.DMA
    vmem = pl.BlockSpec(memory_space=pltpu.VMEM)
    anywhere = pl.BlockSpec(memory_space=pl.ANY)
    places = jnp.transpose(coordinates, (1, 2, 3, 0))

    def sums(n):
        return [
            pltpu.VMEM((tiles, half, width), f32),
            pltpu.VMEM((tiles, n - 1, half, width), bf16),
            pltpu.VMEM((tiles, n - 1, half, width), bf16),
            pltpu.VMEM((half, rank), bf16),
        ]

    def swapped():
        return [pltpu.VMEM((tiles, edge, width), f32), pltpu.VMEM((tiles, half, width), f32)]

    def one_half():
        return [pltpu.VMEM((tiles, half, width), bf16)] * 2

    scratch = [
        pltpu.VMEM((2, edge, edge, edge), bf16),
        pltpu.VMEM((edge, edge, edge), bf16),
        pltpu.VMEM((rank, rank), bf16),
        pltpu.VMEM((rank, rank), bf16),
        (pltpu.VMEM((na, nc, hr, rank // parts), bf16),) * parts,
        pltpu.VMEM((nb, nc, hr, rank), bf16),
        pltpu.VMEM((nb, nc, hr, rank), bf16),
        (pltpu.VMEM((na, rs, width), bf16),) * tiles,
        *one_half(),
        (pltpu.VMEM((nb, edge, width), bf16),) * tiles,
        pltpu.VMEM((tiles, edge, width), f32),
        pltpu.VMEM((tiles, edge + half, width), f32),
        pltpu.VMEM((tiles, edge + half, width), f32),
        pltpu.VMEM((tiles, half, width), f32),
        pltpu.VMEM((edge + half, rank), bf16),
        *swapped(),
        *sums(na),
        pltpu.SMEM(places.shape, jnp.int32),
        pltpu.SMEM(occupancy.shape, jnp.int32),
        pltpu.SMEM((nb, nc, 8), jnp.int32),
        dma((parts + tiles + 5,)),
        dma((2,)),
        dma((2, nb, nc)),
        dma((2, parts, na, nc)),
        dma((2, 2, max(parts, tiles))),
        dma((2, parts, nb, nc)),
        dma((2, tiles, na - 1)),
        dma((2, tiles, nb - 1)),
        dma((2, tiles, na - 1)),
        dma((2, 3, tiles)),
    ]
    return pl.pallas_call(
        functools.partial(pair_kernel, sizes),
        name="als_pair",
        out_shape=(
            jax.ShapeDtypeStruct((1, half, rank), bf16),
            jax.ShapeDtypeStruct((1, half, rank), bf16),
        ),
        in_specs=[anywhere, anywhere, anywhere, vmem, vmem, anywhere, anywhere],
        out_specs=(vmem, vmem),
        scratch_shapes=scratch,
        compiler_params=pltpu.CompilerParams(
            collective_id=0, has_side_effects=True, vmem_limit_bytes=VMEM_LIMIT
        ),
    )(blocks, places, occupancy, second_factor, third_factor, inverse_first, inverse_second)


def pairs_fit(sizes, blocks, second_factor, third_factor):
    na, nb, nc = sizes
    edge = blocks.shape[-1]
    third_rows = third_factor.shape[1]
    return (
        nc == 2
        and na == JB
        and nb == IB
        and second_factor.shape[1] * nc == edge
        and third_rows * nb == edge
        and third_rows % (16 * nc) == 0
    )


def general_call(
    sizes,
    blocks,
    coordinates,
    occupancy,
    second_factor,
    third_factor,
    inverse_first,
    inverse_second,
):
    na, nb, nc = sizes
    edge, rank = blocks.shape[-1], inverse_first.shape[0]
    tiles = TILES
    width = rank // tiles
    rs, rt = second_factor.shape[1], third_factor.shape[1]
    sh1, sh2 = IB * edge // (nb * nc), JB * edge // (na * nc)
    bf16, f32 = jnp.bfloat16, jnp.float32
    dma = pltpu.SemaphoreType.DMA
    widest_k = max(nc - 1, 1)
    vmem = pl.BlockSpec(memory_space=pltpu.VMEM)
    anywhere = pl.BlockSpec(memory_space=pl.ANY)
    scratch = [
        pltpu.VMEM((2, edge, edge, edge), bf16),
        pltpu.VMEM((rank, rank), bf16),
        pltpu.VMEM((rank, rank), bf16),
        pltpu.VMEM((IB + JB, width), f32),
        pltpu.VMEM((IB + JB, width), f32),
        pltpu.VMEM((tiles, na, nb, rt, width), bf16),
        pltpu.VMEM((tiles, na, nc, rs, width), bf16),
        pltpu.VMEM((tiles, edge, width), bf16),
        pltpu.VMEM((tiles, edge, width), bf16),
        pltpu.VMEM((edge, width), bf16),
        pltpu.VMEM((edge, width), f32),
        pltpu.VMEM((tiles, edge, edge, width), bf16),
        pltpu.VMEM((edge, width), f32),
        pltpu.VMEM((tiles, nc - 1, nb, sh1, width), bf16),
        pltpu.VMEM((tiles, nc - 1, nb, sh1, width), bf16),
        pltpu.VMEM((tiles, nb, sh1, width), f32),
        pltpu.VMEM((tiles, nb - 1, sh1, width), bf16),
        pltpu.VMEM((tiles, nb - 1, sh1, width), bf16),
        pltpu.VMEM((tiles, sh1, width), f32),
        pltpu.VMEM((sh1, rank), bf16),
        pltpu.VMEM((tiles, nb, nc, sh1, width), bf16),
        pltpu.VMEM((tiles, nc - 1, na, sh2, width), bf16),
        pltpu.VMEM((tiles, nc - 1, na, sh2, width), bf16),
        pltpu.VMEM((tiles, na, sh2, width), f32),
        pltpu.VMEM((tiles, na - 1, sh2, width), bf16),
        pltpu.VMEM((tiles, na - 1, sh2, width), bf16),
        pltpu.VMEM((tiles, sh2, width), f32),
        pltpu.VMEM((sh2, rank), bf16),
        pltpu.SMEM(coordinates.shape, jnp.int32),
        pltpu.SMEM(occupancy.shape, jnp.int32),
        dma((2 * tiles + 5,)),
        dma((2,)),
        dma((2,)),
        dma((3, tiles, na - 1)),
        dma((3, tiles, na - 1)),
        dma((3, tiles, nb - 1)),
        dma((3, tiles, nb - 1)),
        dma((5, tiles, widest_k)),
        dma((5, tiles, widest_k)),
    ]
    return pl.pallas_call(
        functools.partial(kernel, sizes),
        name="als",
        out_shape=(
            jax.ShapeDtypeStruct((1, sh1, rank), bf16),
            jax.ShapeDtypeStruct((1, sh2, rank), bf16),
        ),
        in_specs=[anywhere, anywhere, anywhere, vmem, vmem, anywhere, anywhere],
        out_specs=(vmem, vmem),
        scratch_shapes=scratch,
        compiler_params=pltpu.CompilerParams(
            collective_id=0, has_side_effects=True, vmem_limit_bytes=67043328
        ),
    )(blocks, coordinates, occupancy, second_factor, third_factor, inverse_first, inverse_second)


def body(sizes, *args):
    blocks, second_factor, third_factor = args[0], args[3], args[4]
    vmem = pl.BlockSpec(memory_space=pltpu.VMEM)
    call = pair_call if pairs_fit(sizes, blocks, second_factor, third_factor) else general_call
    results = call(sizes, *args)
    return pl.pallas_call(
        hand_over,
        name="hand_over",
        out_shape=tuple(jax.ShapeDtypeStruct(x.shape, x.dtype) for x in results),
        in_specs=[vmem, vmem],
        out_specs=(vmem, vmem),
    )(*results)


def hand_over(first_in, second_in, first_out, second_out):
    first_out[...] = first_in[...]
    second_out[...] = second_in[...]


def solution(mesh):
    sizes = tuple(mesh.shape[name] for name in AXES)
    in_specs = (
        P("ia", "ja", "ka", None, None, None),
        P(None, "ia", "ja", "ka"),
        P("ia", "ja", "ka"),
        P("ja", ("ia", "ka"), None),
        P("ka", ("ia", "ja"), None),
        P(),
        P(),
    )
    out_specs = (P("ia", ("ja", "ka"), None), P("ja", ("ia", "ka"), None))
    return jax.shard_map(
        functools.partial(body, sizes),
        mesh=mesh,
        in_specs=in_specs,
        out_specs=out_specs,
        check_vma=False,
    )
```

```python
import functools

import jax
import jax.numpy as jnp
from jax import lax
from jax.experimental import pallas as pl
from jax.experimental.pallas import tpu as pltpu
from jax.sharding import PartitionSpec as P

IB = 4
JB = 4
TILES = 4
PAIR_TILES = 2
PARTS = 1
VMEM_LIMIT = 67043328
MESH = pl.DeviceIdType.MESH
AXES = ("ia", "ja", "ka")


def kernel(
    sizes,
    blocks,
    places_in,
    occupied_in,
    second_in,
    third_in,
    inverse_first,
    inverse_second,
    first_out,
    second_out,
    xbuf,
    inv1,
    inv2,
    meta_s,
    meta_r,
    cbuf,
    bbuf,
    slab_s,
    slab_r,
    cuse,
    buse,
    tbuf,
    oacc,
    d1s,
    d1r,
    keep1,
    p1s,
    p1r,
    own1,
    fr1,
    abuf,
    d2s,
    d2r,
    keep2,
    p2s,
    p2r,
    own2,
    fr2,
    places,
    occupied,
    local_sem,
    once_send,
    once_recv,
    z_send,
    z_recv,
    y_send,
    y_recv,
    k_send,
    k_recv,
):
    na, nb, nc = sizes
    tiles, edge, width = slab_s.shape
    rs, rt = bbuf.shape[3], cbuf.shape[3]
    sh1, sh2 = abuf.shape[3], own2.shape[1]
    a, b, c = (lax.axis_index(name) for name in AXES)
    sent = []

    def away(axis, d):
        n = sizes[AXES.index(axis)]
        me = (a, b, c)[AXES.index(axis)]
        return lax.rem(me + d, n)

    def send(src, dst, send_sem, recv_sem, axis, d):
        copy = pltpu.make_async_remote_copy(
            src_ref=src,
            dst_ref=dst,
            send_sem=send_sem,
            recv_sem=recv_sem,
            device_id={axis: away(axis, d)},
            device_id_type=MESH,
        )
        copy.start()
        sent.append(copy)
        return copy

    def cols(t):
        return pl.ds(t * width, width)

    local = []

    def local_copy(src, dst):
        copy = pltpu.make_async_copy(src, dst, local_sem.at[len(local)])
        copy.start()
        local.append(copy)
        return copy

    got_places = local_copy(places_in, places)
    got_occupied = local_copy(occupied_in, occupied)
    own_third = [
        local_copy(third_in.at[0, :, cols(t)], cbuf.at[t, a, b]) for t in range(tiles)
    ]
    own_second = [
        local_copy(second_in.at[0, :, cols(t)], bbuf.at[t, a, c]) for t in range(tiles)
    ]
    own_block = local_copy(blocks.at[0, 0, 0], xbuf.at[0])
    got_inv1 = local_copy(inverse_first, inv1)
    got_inv2 = local_copy(inverse_second, inv2)

    barrier = pltpu.get_barrier_semaphore()
    for axis, n in zip(AXES, sizes):
        for d in range(1, n):
            pl.semaphore_signal(
                barrier, inc=1, device_id={axis: away(axis, d)}, device_id_type=MESH
            )
    got_places.wait()
    got_occupied.wait()
    keep = occupied[0, 0, 0] > 0
    row0, col0, layer0 = (places[m, 0, 0, 0] for m in range(3))
    row1, col1, layer1 = (places[m, 0, 0, 1] for m in range(3))
    weight1 = jnp.where(occupied[0, 0, 1] > 0, 1.0, 0.0).astype(jnp.float32)
    for q in range(IB):
        value = jnp.where(row1 == q, weight1, 0.0)
        meta_s[pl.ds(q, 1), :] = jnp.full((1, width), value, jnp.float32)
    for q in range(JB):
        value = jnp.where(col1 == q, weight1, 0.0)
        meta_s[pl.ds(IB + q, 1), :] = jnp.full((1, width), value, jnp.float32)
    pl.semaphore_wait(barrier, (na - 1) + (nb - 1) + (nc - 1))

    def chosen(own_value, row):
        own = jnp.where(own_value, 1.0, 0.0).astype(jnp.float32)
        return jnp.where(keep, jnp.full((1, width), own, jnp.float32), meta_r[pl.ds(row, 1), :]) > 0.5

    def third_column(t):
        return [
            send(
                third_in.at[0, :, cols(t)],
                cbuf.at[t, a, b],
                z_send.at[0, t, d - 1],
                z_recv.at[0, t, d - 1],
                "ia",
                d,
            )
            for d in range(1, na)
        ]

    def second_column(t):
        return [
            send(
                second_in.at[0, :, cols(t)],
                bbuf.at[t, a, c],
                z_send.at[1, t, d - 1],
                z_recv.at[1, t, d - 1],
                "ia",
                d,
            )
            for d in range(1, na)
        ]

    third_z, second_z = {}, {}
    third_z[0] = third_column(0)
    block_copy = send(blocks.at[0, 0, 1], xbuf.at[1], once_send.at[0], once_recv.at[0], "ka", 1)
    meta_copy = send(meta_s, meta_r, once_send.at[1], once_recv.at[1], "ka", 1)
    for t in range(1, tiles):
        third_z[t] = third_column(t)
        second_z[t - 1] = second_column(t - 1)
    second_z[tiles - 1] = second_column(tiles - 1)

    third_y, second_k, slab_copy = {}, {}, {}

    def spread_third(t):
        own_third[t].wait()
        for copy in third_z[t]:
            copy.wait_recv()
        third_y[t] = [
            send(
                cbuf.at[t, :, b],
                cbuf.at[t, :, b],
                y_send.at[0, t, d - 1],
                y_recv.at[0, t, d - 1],
                "ja",
                d,
            )
            for d in range(1, nb)
        ]

    def spread_second(t):
        own_second[t].wait()
        for copy in second_z[t]:
            copy.wait_recv()
        second_k[t] = [
            send(
                bbuf.at[t, :, c],
                bbuf.at[t, :, c],
                k_send.at[0, t, d - 1],
                k_recv.at[0, t, d - 1],
                "ka",
                d,
            )
            for d in range(1, nc)
        ]

    def layer_piece(t, layer, piece):
        per = edge // rt
        total = na * nb * rt // edge
        value = None
        for q in range(total):
            s = q * per + piece
            rows = cbuf[t, s // nb, s % nb]
            value = rows if value is None else jnp.where(layer == q, rows, value)
        return value

    def pass_slab(t):
        for copy in third_y[t]:
            copy.wait_recv()
        for piece in range(edge // rt):
            slab_s[t, pl.ds(piece * rt, rt), :] = layer_piece(t, layer1, piece)
        slab_copy[t] = send(
            slab_s.at[t], slab_r.at[t], k_send.at[1, t, 0], k_recv.at[1, t, 0], "ka", 1
        )
        for piece in range(edge // rt):
            cuse[pl.ds(piece * rt, rt), :] = layer_piece(t, layer0, piece)

    def first_products(t):
        for copy in second_k[t]:
            copy.wait_recv()
        if t == 0:
            own_block.wait()
            block_copy.wait_recv()
            meta_copy.wait_recv()
        masks = [chosen(col0 == q, IB + q) for q in range(JB)]
        per = edge // rs
        for piece in range(per):
            value = jnp.zeros((rs, width), jnp.float32)
            for q in range(JB):
                s = q * per + piece
                rows = bbuf[t, s // nc, s % nc].astype(jnp.float32)
                value = jnp.where(masks[q], rows, value)
            buse[pl.ds(piece * rs, rs), :] = value
        slab_copy[t].wait_recv()
        cuse[...] = jnp.where(keep, cuse[...], slab_r[t])
        slot = jnp.where(keep, 0, 1)

        def eight(step, carry):
            base = pl.multiple_of(step * 8, 8)
            sums = []
            for u in range(8):
                product = jnp.dot(
                    xbuf[slot, base + u], cuse[...], preferred_element_type=jnp.float32
                )
                tbuf[t, base + u] = product.astype(jnp.bfloat16)
                sums.append(jnp.sum(product * buse[...], axis=0, keepdims=True))
            oacc[pl.ds(base, 8), :] = jnp.concatenate(sums, axis=0)
            return carry

        lax.fori_loop(0, edge // 8, eight, 0)

    def owned_piece(owner, rows, own_place, meta_row):
        start = owner * rows
        block = start // edge
        off = pl.multiple_of(start % edge, rows)
        mask = chosen(own_place == block, meta_row + block)
        return jnp.where(mask, oacc[pl.ds(off, rows), :], 0.0)

    def pair_sums(t, n, rows, own_place, meta_row, outgoing, arriving, kept, kind):
        copies = []
        for d in range(1, nc):
            for m in range(n):
                owner = m * nc + away("ka", d)
                outgoing[t, d - 1, m] = owned_piece(owner, rows, own_place, meta_row).astype(
                    jnp.bfloat16
                )
            copies.append(
                send(
                    outgoing.at[t, d - 1],
                    arriving.at[t, d - 1],
                    k_send.at[kind, t, d - 1],
                    k_recv.at[kind, t, d - 1],
                    "ka",
                    d,
                )
            )
        for m in range(n):
            kept[t, m] = owned_piece(m * nc + c, rows, own_place, meta_row)
        return copies

    def chip_sums(t, axis, n, copies, arriving, kept, outgoing, landing, own, sends, recvs, kind):
        for copy in copies:
            copy.wait_recv()
        started = []
        for d in range(n):
            m = away(axis, d)
            value = kept[t, m]
            for e in range(1, nc):
                value = value + arriving[t, e - 1, m].astype(jnp.float32)
            if d == 0:
                own[t] = value
            else:
                outgoing[t, d - 1] = value.astype(jnp.bfloat16)
                started.append(
                    send(
                        outgoing.at[t, d - 1],
                        landing.at[t, d - 1],
                        sends.at[kind, t, d - 1],
                        recvs.at[kind, t, d - 1],
                        axis,
                        d,
                    )
                )
        return started

    first_k, first_y = {}, {}

    def first_chip_sums(t):
        first_y[t] = chip_sums(
            t, "ja", nb, first_k[t], d1r, keep1, p1s, p1r, own1, y_send, y_recv, 1
        )

    spread_third(0)
    spread_second(0)
    for t in range(tiles):
        if t + 1 < tiles:
            spread_third(t + 1)
        pass_slab(t)
        if t:
            first_chip_sums(t - 1)
        first_products(t)
        first_k[t] = pair_sums(t, nb, sh1, row0, 0, d1s, d1r, keep1, 2)
        if t + 1 < tiles:
            spread_second(t + 1)
    first_chip_sums(tiles - 1)

    def gathered(t, copies, own, landing, n):
        for copy in copies:
            copy.wait_recv()
        value = own[t]
        for d in range(1, n):
            value = value + landing[t, d - 1].astype(jnp.float32)
        return value.astype(jnp.bfloat16)

    for t in range(tiles):
        fr1[:, cols(t)] = gathered(t, first_y[t], own1, p1r, nb)
    got_inv1.wait()
    new_y, new_k = {}, {}
    for t in range(tiles):
        value = jnp.dot(fr1[...], inv1[:, cols(t)], preferred_element_type=jnp.float32)
        value = value.astype(jnp.bfloat16)
        abuf[t, b, c] = value
        first_out[0, :, cols(t)] = value
        new_y[t] = [
            send(
                abuf.at[t, b, c],
                abuf.at[t, b, c],
                y_send.at[2, t, d - 1],
                y_recv.at[2, t, d - 1],
                "ja",
                d,
            )
            for d in range(1, nb)
        ]

    def spread_new(t):
        for copy in new_y[t]:
            copy.wait_recv()
        new_k[t] = [
            send(
                abuf.at[t, :, c],
                abuf.at[t, :, c],
                k_send.at[3, t, d - 1],
                k_recv.at[3, t, d - 1],
                "ka",
                d,
            )
            for d in range(1, nc)
        ]

    def second_products(t):
        for copy in new_k[t]:
            copy.wait_recv()
        masks = [chosen(row0 == q, q) for q in range(IB)]
        per = edge // sh1
        for piece in range(per):
            value = jnp.zeros((sh1, width), jnp.float32)
            for q in range(IB):
                s = q * per + piece
                rows = abuf[t, s // nc, s % nc].astype(jnp.float32)
                value = jnp.where(masks[q], rows, value)
            buse[pl.ds(piece * sh1, sh1), :] = value
        lanes = 128
        for lane in range(0, width, lanes):

            def eight(step, total):
                base = pl.multiple_of(step * 8, 8)
                rows = buse[pl.ds(base, 8), pl.ds(lane, lanes)]
                for u in range(8):
                    total = total + rows[u : u + 1] * tbuf[t, base + u, :, pl.ds(lane, lanes)].astype(
                        jnp.float32
                    )
                return total

            oacc[:, pl.ds(lane, lanes)] = lax.fori_loop(
                0, edge // 8, eight, jnp.zeros((edge, lanes), jnp.float32)
            )

    second_s, second_y = {}, {}

    def second_chip_sums(t):
        second_y[t] = chip_sums(
            t, "ia", na, second_s[t], d2r, keep2, p2s, p2r, own2, z_send, z_recv, 2
        )

    spread_new(0)
    for t in range(tiles):
        if t + 1 < tiles:
            spread_new(t + 1)
        second_products(t)
        second_s[t] = pair_sums(t, na, sh2, col0, IB, d2s, d2r, keep2, 4)
        if t:
            second_chip_sums(t - 1)
    second_chip_sums(tiles - 1)
    for t in range(tiles):
        fr2[:, cols(t)] = gathered(t, second_y[t], own2, p2r, na)
    got_inv2.wait()
    for t in range(tiles):
        value = jnp.dot(fr2[...], inv2[:, cols(t)], preferred_element_type=jnp.float32)
        second_out[0, :, cols(t)] = value.astype(jnp.bfloat16)
    for copy in sent:
        copy.wait_send()


def pair_kernel(
    sizes,
    blocks,
    places_in,
    occupied_in,
    second_in,
    third_in,
    inverse_first,
    inverse_second,
    first_out,
    second_out,
    xbuf,
    xturn,
    inv1,
    inv2,
    tz,
    ts,
    cg,
    bz,
    bs,
    br,
    pb,
    mine1,
    xs,
    xr,
    own1,
    fr1,
    sacc,
    srecv,
    own2,
    p2s,
    p2r,
    fr2,
    places,
    occupied,
    meta,
    local_sem,
    block_sem,
    meta_sems,
    tz_sems,
    far_sems,
    ts_sems,
    bz_sems,
    p1_sems,
    p2_sems,
    pair_sems,
):
    na, nb, nc = sizes
    tiles, rs, width = bs.shape
    parts, edge = tz_sems.shape[1], xbuf.shape[1]
    hr, wide = tz[0].shape[2:]
    half = edge // nc
    bf16, f32 = jnp.bfloat16, jnp.float32
    a, b, c = (lax.axis_index(name) for name in AXES)
    other = 1 - c
    sent, maybe_sent = [], []

    def send(src, dst, sems, place, **device_id):
        copy = pltpu.make_async_remote_copy(
            src_ref=src,
            dst_ref=dst,
            send_sem=sems.at[(0, *place)],
            recv_sem=sems.at[(1, *place)],
            device_id=device_id,
            device_id_type=MESH,
        )
        copy.start()
        sent.append(copy)
        return copy

    def arrival(dst, sem):
        return pltpu.make_async_remote_copy(
            src_ref=dst, dst_ref=dst, send_sem=sem, recv_sem=sem, device_id={"ka": other}, device_id_type=MESH
        )

    first, last = a == 0, a == na - 1
    inner = jnp.logical_and(a > 0, a < na - 1)
    far_piece = jnp.where(a == 1, na - 1, 0)
    far_dest = jnp.where(a == 1, 0, na - 1)

    def reaches(d):
        return jnp.logical_not(last if d == 1 else first) if d in (1, na - 1) else None

    def hears(d):
        return jnp.logical_not(first if d == 1 else last) if d in (1, na - 1) else None

    def under(condition, function):
        if condition is None:
            function()
        else:
            pl.when(condition)(function)

    def send_if(condition, src, dst, sems, place, **device_id):
        copy = pltpu.make_async_remote_copy(
            src_ref=src,
            dst_ref=dst,
            send_sem=sems.at[(0, *place)],
            recv_sem=sems.at[(1, *place)],
            device_id=device_id,
            device_id_type=MESH,
        )
        under(condition, copy.start)
        maybe_sent.append((condition, copy))

    def cols(t):
        return pl.ds(t * width, width)

    def wides(t):
        return pl.ds(t * wide, wide)

    def turn(me, d, n):
        return lax.rem(me + d, n)

    local = []

    def local_copy(src, dst):
        copy = pltpu.make_async_copy(src, dst, local_sem.at[len(local)])
        copy.start()
        local.append(copy)
        return copy

    def third_half(p, t):
        return third_in.at[0, pl.ds(pl.multiple_of(p * hr, hr), hr), wides(t)]

    barrier = pltpu.get_barrier_semaphore()
    peers = [{"ia": turn(a, d, na), "ka": turn(c, e, nc)} for d in range(na) for e in range(nc) if d or e]
    peers += [{"ja": turn(b, d, nb), "ka": turn(c, e, nc)} for d in range(1, nb) for e in range(nc)]
    for peer in peers:
        pl.semaphore_signal(barrier, inc=1, device_id=peer, device_id_type=MESH)

    got_places = local_copy(places_in, places)
    got_occupied = local_copy(occupied_in, occupied)
    own_third = [local_copy(third_half(c, t), tz[t].at[a, c]) for t in range(parts)]
    own_second = [local_copy(second_in.at[0, :, cols(t)], bz[t].at[a]) for t in range(tiles)]
    own_block = local_copy(blocks.at[0, 0, 0], xbuf.at[0])
    got_inv1 = local_copy(inverse_first, inv1)
    got_inv2 = local_copy(inverse_second, inv2)
    got_places.wait()
    got_occupied.wait()
    for slot in range(2):
        for m in range(3):
            meta[b, c, 4 * slot + m] = places[0, 0, slot, m]
        meta[b, c, 4 * slot + 3] = occupied[0, 0, slot]
    pl.semaphore_wait(barrier, len(peers))

    def third_column(t):
        for d in [*range(1, na), 0]:
            for e in range(nc):
                if d or e:
                    send_if(
                        reaches(d),
                        third_half(turn(c, e, nc), t),
                        tz[t].at[a, c],
                        tz_sems,
                        (t, d, e),
                        ia=turn(a, d, na),
                        ka=turn(c, e, nc),
                    )

    def third_near(t):
        own_third[t].wait()
        for d in [*range(1, na), 0]:
            for e in range(nc):
                if d or e:
                    under(hears(d), arrival(tz[t].at[a, c], tz_sems.at[1, t, d, e]).wait_recv)
        send_if(inner, tz[t].at[far_piece], tz[t].at[far_piece], far_sems, (0, t), ia=far_dest)

    def third_far(t):
        far = arrival(tz[t].at[na - 1], far_sems.at[1, 0, t])
        under(jnp.logical_not(inner), far.wait_recv)

    def second_column(t):
        for d in range(1, na):
            send_if(
                reaches(d),
                second_in.at[0, :, cols(t)],
                bz[t].at[a],
                bz_sems,
                (t, d - 1),
                ia=turn(a, d, na),
            )

    def second_near(t):
        own_second[t].wait()
        for d in range(1, na):
            under(hears(d), arrival(bz[t].at[a], bz_sems.at[1, t, d - 1]).wait_recv)
        send_if(inner, bz[t].at[far_piece], bz[t].at[far_piece], far_sems, (1, t), ia=far_dest)

    def second_far(t):
        far = arrival(bz[t].at[na - 1], far_sems.at[1, 1, t])
        under(jnp.logical_not(inner), far.wait_recv)

    for t in range(parts):
        third_column(t)
    meta_copies = [
        send(
            meta.at[b, c],
            meta.at[b, c],
            meta_sems,
            (d, e),
            ja=turn(b, d, nb),
            ka=turn(c, e, nc),
        )
        for d in range(nb)
        for e in range(nc)
        if d or e
    ]
    block_copy = send(blocks.at[0, 0, 1], xbuf.at[1], block_sem, (), ka=other)
    second_column(0)

    for copy in meta_copies:
        copy.wait_recv()

    def work(bb, cc):
        keep = meta[bb, cc, 3] > 0
        row, col, layer = (jnp.where(keep, meta[bb, cc, m], meta[bb, 1 - cc, 4 + m]) for m in range(3))
        return row, col, layer, jnp.where(keep, cc, 1 - cc), jnp.where(keep, 1, meta[bb, 1 - cc, 7])

    row_own, col_own, _, kept, valid_own = work(b, c)
    row_oth, col_oth, _, _, valid_oth = work(b, other)
    slot = jnp.where(kept == c, 0, 1)

    third_y = {}

    def pass_third(t):
        third_far(t)
        copies = []
        for d in range(nb):
            for e in range(nc):
                bb, cc = turn(b, d, nb), turn(c, e, nc)
                _, _, layer, span, _ = work(bb, cc)
                rows = tz[t][layer, span]
                if d or e:
                    ts[d, e, :, wides(t)] = rows
                    copies.append(
                        send(
                            ts.at[d, e, :, wides(t)],
                            cg.at[b, c, :, wides(t)],
                            ts_sems,
                            (t, d, e),
                            ja=bb,
                            ka=cc,
                        )
                    )
                else:
                    cg[b, c, :, wides(t)] = rows
        third_y[t] = copies

    ahead = [*range(1, tiles)]

    def more():
        if ahead:
            second_column(ahead.pop(0))

    for t in range(parts):
        third_near(t)
        more()
        pass_third(t)
    second_near(0)
    more()

    own_block.wait()
    block_copy.wait_recv()

    sub = 16

    def swap(step, carry):
        i0 = pl.multiple_of(step // (edge // sub) * sub, sub)
        j0 = pl.multiple_of(step % (edge // sub) * sub, sub)
        piece = xbuf[slot, pl.ds(i0, sub), pl.ds(j0, sub), :]
        xturn[pl.ds(j0, sub), pl.ds(i0, sub), :] = jnp.swapaxes(piece, 0, 1)
        return carry

    lax.fori_loop(0, (edge // sub) ** 2, swap, 0)

    def layers(t):
        return cg[:, :, :, cols(t)].reshape(edge, width)

    def halves(own, received):
        low = jnp.where(c == 0, own, received)
        high = jnp.where(c == 0, received, own)
        return jnp.concatenate([low, high], axis=0)

    def product(rows, layer_rows, pages):
        left = jnp.concatenate(pages, axis=1)
        right = jnp.concatenate([rows[u : u + 1] * layer_rows for u in range(edge)], axis=0)
        return jnp.dot(left, right, preferred_element_type=f32)

    own_rows = pl.ds(pl.multiple_of(c * half, half), half)
    other_rows = pl.ds(pl.multiple_of(other * half, half), half)

    def swap_half(t, acc, received, kind):
        return send(acc.at[t, other_rows], received.at[t], pair_sems, (kind, t), ka=other)

    def buckets(t, copy, acc, received, place_own, place_oth, me, axis, n, own, outgoing, landing, sems):
        copy.wait_recv()
        mine, theirs = acc[t, own_rows], received[t]
        copies = []
        for d in [*range(1, n), 0]:
            q = turn(me, d, n)
            value = jnp.where((place_own == q) & (valid_own > 0), mine, 0.0) + jnp.where(
                (place_oth == q) & (valid_oth > 0), theirs, 0.0
            )
            if d:
                outgoing[t, d - 1] = value.astype(bf16)
                copies.append(
                    send(outgoing.at[t, d - 1], landing.at[t, d - 1], sems, (t, d - 1), **{axis: q})
                )
            else:
                own[t] = value
        return copies

    def gathered(t, copies, own, landing, n):
        for copy in copies:
            copy.wait_recv()
        value = own[t]
        for d in range(1, n):
            value = value + landing[t, d - 1].astype(f32)
        return value.astype(bf16)

    second_k, first_y, first_k, second_s, second_y = {}, {}, {}, {}, {}
    in_plane = [work(bb, c) for bb in range(nb)]

    def pass_second(t):
        second_far(t)
        bs[t] = bz[t][col_oth]
        second_k[t] = send(bs.at[t], br.at[t], pair_sems, (0, t), ka=other)

    def first_products(t):
        second_k[t].wait_recv()
        sums = product(halves(bz[t][col_own], br[t]), layers(t), [xturn[j] for j in range(edge)])
        pb[t][b] = sums.astype(bf16)
        first_y[t] = [
            send(pb[t].at[b], pb[t].at[b], p1_sems, (t, d - 1), ja=turn(b, d, nb))
            for d in range(1, nb)
        ]

    def first_sums(t):
        for copy in first_y[t]:
            copy.wait_recv()

        def rows_of(place, rows):
            total = None
            for bb in range(nb):
                row, _, _, _, valid = in_plane[bb]
                chosen = jnp.logical_and(row == place, valid > 0)
                value = jnp.where(chosen, pb[t][bb, rows].astype(f32), 0.0)
                total = value if total is None else total + value
            return total

        xs[t, pl.ds(0, edge)] = rows_of(row_oth, pl.ds(0, edge))
        xs[t, pl.ds(edge, half)] = rows_of(b, other_rows)
        first_k[t] = send(xs.at[t], xr.at[t], pair_sems, (1, t), ka=other)
        mine1[t] = rows_of(row_own, pl.ds(0, edge))
        own1[t] = rows_of(b, own_rows)

    def first_rows(t):
        first_k[t].wait_recv()
        fr1[pl.ds(0, edge), cols(t)] = (mine1[t] + xr[t, pl.ds(0, edge)]).astype(bf16)
        fr1[pl.ds(edge, half), cols(t)] = (own1[t] + xr[t, pl.ds(edge, half)]).astype(bf16)

    pass_second(0)
    for part in range(parts):
        for copy in third_y[part]:
            copy.wait_recv()
    for t in range(tiles):
        if t + 1 < tiles:
            second_near(t + 1)
            more()
        first_products(t)
        if t + 1 < tiles:
            pass_second(t + 1)
        if t:
            first_sums(t - 1)
        if t > 1:
            first_rows(t - 2)
    first_sums(tiles - 1)
    for t in range(max(tiles - 2, 0), tiles):
        first_rows(t)
    got_inv1.wait()

    def second_buckets(t):
        second_y[t] = buckets(
            t, second_s[t], sacc, srecv, col_own, col_oth, a, "ia", na, own2, p2s, p2r, p2_sems
        )

    for t in range(tiles):
        value = jnp.dot(fr1[...], inv1[:, cols(t)], preferred_element_type=f32).astype(bf16)
        first_out[0, :, cols(t)] = value[edge:]
        if t:
            second_buckets(t - 1)
        sacc[t] = product(value[:edge], layers(t), [xbuf[slot, i] for i in range(edge)])
        second_s[t] = swap_half(t, sacc, srecv, 2)
    second_buckets(tiles - 1)
    for copy in sent:
        copy.wait_send()
    for condition, copy in maybe_sent:
        under(condition, copy.wait_send)
    for t in range(tiles):
        fr2[:, cols(t)] = gathered(t, second_y[t], own2, p2r, na)
    got_inv2.wait()
    for t in range(tiles):
        value = jnp.dot(fr2[...], inv2[:, cols(t)], preferred_element_type=f32)
        second_out[0, :, cols(t)] = value.astype(bf16)


def pair_call(sizes, blocks, coordinates, occupancy, second_factor, third_factor, inverse_first, inverse_second):
    na, nb, nc = sizes
    edge, rank = blocks.shape[-1], inverse_first.shape[0]
    tiles, parts = PAIR_TILES, PARTS
    width = rank // tiles
    rs, hr = second_factor.shape[1], third_factor.shape[1] // nc
    half = edge // nc
    bf16, f32 = jnp.bfloat16, jnp.float32
    dma = pltpu.SemaphoreType.DMA
    vmem = pl.BlockSpec(memory_space=pltpu.VMEM)
    anywhere = pl.BlockSpec(memory_space=pl.ANY)
    places = jnp.transpose(coordinates, (1, 2, 3, 0))

    def sums(n):
        return [
            pltpu.VMEM((tiles, half, width), f32),
            pltpu.VMEM((tiles, n - 1, half, width), bf16),
            pltpu.VMEM((tiles, n - 1, half, width), bf16),
            pltpu.VMEM((half, rank), bf16),
        ]

    def swapped():
        return [pltpu.VMEM((tiles, edge, width), f32), pltpu.VMEM((tiles, half, width), f32)]

    def one_half():
        return [pltpu.VMEM((tiles, half, width), bf16)] * 2

    scratch = [
        pltpu.VMEM((2, edge, edge, edge), bf16),
        pltpu.VMEM((edge, edge, edge), bf16),
        pltpu.VMEM((rank, rank), bf16),
        pltpu.VMEM((rank, rank), bf16),
        (pltpu.VMEM((na, nc, hr, rank // parts), bf16),) * parts,
        pltpu.VMEM((nb, nc, hr, rank), bf16),
        pltpu.VMEM((nb, nc, hr, rank), bf16),
        (pltpu.VMEM((na, rs, width), bf16),) * tiles,
        *one_half(),
        (pltpu.VMEM((nb, edge, width), bf16),) * tiles,
        pltpu.VMEM((tiles, edge, width), f32),
        pltpu.VMEM((tiles, edge + half, width), f32),
        pltpu.VMEM((tiles, edge + half, width), f32),
        pltpu.VMEM((tiles, half, width), f32),
        pltpu.VMEM((edge + half, rank), bf16),
        *swapped(),
        *sums(na),
        pltpu.SMEM(places.shape, jnp.int32),
        pltpu.SMEM(occupancy.shape, jnp.int32),
        pltpu.SMEM((nb, nc, 8), jnp.int32),
        dma((parts + tiles + 5,)),
        dma((2,)),
        dma((2, nb, nc)),
        dma((2, parts, na, nc)),
        dma((2, 2, max(parts, tiles))),
        dma((2, parts, nb, nc)),
        dma((2, tiles, na - 1)),
        dma((2, tiles, nb - 1)),
        dma((2, tiles, na - 1)),
        dma((2, 3, tiles)),
    ]
    return pl.pallas_call(
        functools.partial(pair_kernel, sizes),
        name="als_pair",
        out_shape=(
            jax.ShapeDtypeStruct((1, half, rank), bf16),
            jax.ShapeDtypeStruct((1, half, rank), bf16),
        ),
        in_specs=[anywhere, anywhere, anywhere, vmem, vmem, anywhere, anywhere],
        out_specs=(vmem, vmem),
        scratch_shapes=scratch,
        compiler_params=pltpu.CompilerParams(
            collective_id=0, has_side_effects=True, vmem_limit_bytes=VMEM_LIMIT
        ),
    )(blocks, places, occupancy, second_factor, third_factor, inverse_first, inverse_second)


def pairs_fit(sizes, blocks, second_factor, third_factor):
    na, nb, nc = sizes
    edge = blocks.shape[-1]
    third_rows = third_factor.shape[1]
    return (
        nc == 2
        and na == JB
        and nb == IB
        and second_factor.shape[1] * nc == edge
        and third_rows * nb == edge
        and third_rows % (16 * nc) == 0
    )


def general_call(
    sizes,
    blocks,
    coordinates,
    occupancy,
    second_factor,
    third_factor,
    inverse_first,
    inverse_second,
):
    na, nb, nc = sizes
    edge, rank = blocks.shape[-1], inverse_first.shape[0]
    tiles = TILES
    width = rank // tiles
    rs, rt = second_factor.shape[1], third_factor.shape[1]
    sh1, sh2 = IB * edge // (nb * nc), JB * edge // (na * nc)
    bf16, f32 = jnp.bfloat16, jnp.float32
    dma = pltpu.SemaphoreType.DMA
    widest_k = max(nc - 1, 1)
    vmem = pl.BlockSpec(memory_space=pltpu.VMEM)
    anywhere = pl.BlockSpec(memory_space=pl.ANY)
    scratch = [
        pltpu.VMEM((2, edge, edge, edge), bf16),
        pltpu.VMEM((rank, rank), bf16),
        pltpu.VMEM((rank, rank), bf16),
        pltpu.VMEM((IB + JB, width), f32),
        pltpu.VMEM((IB + JB, width), f32),
        pltpu.VMEM((tiles, na, nb, rt, width), bf16),
        pltpu.VMEM((tiles, na, nc, rs, width), bf16),
        pltpu.VMEM((tiles, edge, width), bf16),
        pltpu.VMEM((tiles, edge, width), bf16),
        pltpu.VMEM((edge, width), bf16),
        pltpu.VMEM((edge, width), f32),
        pltpu.VMEM((tiles, edge, edge, width), bf16),
        pltpu.VMEM((edge, width), f32),
        pltpu.VMEM((tiles, nc - 1, nb, sh1, width), bf16),
        pltpu.VMEM((tiles, nc - 1, nb, sh1, width), bf16),
        pltpu.VMEM((tiles, nb, sh1, width), f32),
        pltpu.VMEM((tiles, nb - 1, sh1, width), bf16),
        pltpu.VMEM((tiles, nb - 1, sh1, width), bf16),
        pltpu.VMEM((tiles, sh1, width), f32),
        pltpu.VMEM((sh1, rank), bf16),
        pltpu.VMEM((tiles, nb, nc, sh1, width), bf16),
        pltpu.VMEM((tiles, nc - 1, na, sh2, width), bf16),
        pltpu.VMEM((tiles, nc - 1, na, sh2, width), bf16),
        pltpu.VMEM((tiles, na, sh2, width), f32),
        pltpu.VMEM((tiles, na - 1, sh2, width), bf16),
        pltpu.VMEM((tiles, na - 1, sh2, width), bf16),
        pltpu.VMEM((tiles, sh2, width), f32),
        pltpu.VMEM((sh2, rank), bf16),
        pltpu.SMEM(coordinates.shape, jnp.int32),
        pltpu.SMEM(occupancy.shape, jnp.int32),
        dma((2 * tiles + 5,)),
        dma((2,)),
        dma((2,)),
        dma((3, tiles, na - 1)),
        dma((3, tiles, na - 1)),
        dma((3, tiles, nb - 1)),
        dma((3, tiles, nb - 1)),
        dma((5, tiles, widest_k)),
        dma((5, tiles, widest_k)),
    ]
    return pl.pallas_call(
        functools.partial(kernel, sizes),
        name="als",
        out_shape=(
            jax.ShapeDtypeStruct((1, sh1, rank), bf16),
            jax.ShapeDtypeStruct((1, sh2, rank), bf16),
        ),
        in_specs=[anywhere, anywhere, anywhere, vmem, vmem, anywhere, anywhere],
        out_specs=(vmem, vmem),
        scratch_shapes=scratch,
        compiler_params=pltpu.CompilerParams(
            collective_id=0, has_side_effects=True, vmem_limit_bytes=67043328
        ),
    )(blocks, coordinates, occupancy, second_factor, third_factor, inverse_first, inverse_second)


def body(sizes, *args):
    blocks, second_factor, third_factor = args[0], args[3], args[4]
    vmem = pl.BlockSpec(memory_space=pltpu.VMEM)
    call = pair_call if pairs_fit(sizes, blocks, second_factor, third_factor) else general_call
    results = call(sizes, *args)
    return pl.pallas_call(
        hand_over,
        name="hand_over",
        out_shape=tuple(jax.ShapeDtypeStruct(x.shape, x.dtype) for x in results),
        in_specs=[vmem, vmem],
        out_specs=(vmem, vmem),
    )(*results)


def hand_over(first_in, second_in, first_out, second_out):
    first_out[...] = first_in[...]
    second_out[...] = second_in[...]


def solution(mesh):
    sizes = tuple(mesh.shape[name] for name in AXES)
    in_specs = (
        P("ia", "ja", "ka", None, None, None),
        P(None, "ia", "ja", "ka"),
        P("ia", "ja", "ka"),
        P("ja", ("ia", "ka"), None),
        P("ka", ("ia", "ja"), None),
        P(),
        P(),
    )
    out_specs = (P("ia", ("ja", "ka"), None), P("ja", ("ia", "ka"), None))
    return jax.shard_map(
        functools.partial(body, sizes),
        mesh=mesh,
        in_specs=in_specs,
        out_specs=out_specs,
        check_vma=False,
    )
```
